256 devices in a mesh: view: 4 (over y), sent: 32 (over x, z), col: 2 (over core).
Axes of the slice: x: 4, y: 4, z: 8, core: 2. Of those that a mesh axis runs over, the one named last changes fastest.
Arguments:
- sketched: bfloat16 [12, 32768, 2048], P('view', 'sent', 'col')
- widths: int32 [12], P('view'), may hold values from 256 to 2048, as said below
- inv_factor: float32 [12, 2048, 2048], P('view', 'sent', 'col'), as said below
- shared: bfloat16 [32768, 256], P('sent'), may hold values from -6 to 6
Outputs:
- loadings: float32 [12, 2048, 256], P('view', 'col')
- updated: float32 [32768, 256], P('sent')
The draws below stay inside these ranges and needn't reach their ends.
Inputs may be any that keep to these rules, and one draw needn't show every extreme that they name: `widths`: every width is a multiple of 128; in every draw one view has width 2048 and another 2 * 128. Each inv_factor[j] is lower triangular with diagonal entries of 1 to 2.
All inputs are finite; a program needn't handle non-finite values.
Results may differ from the reference program's by a relative error of at most 0.0026.
Values sent between devices are 32-bit elements; how exact they have to be, the bound alone decides.
A program may use at most 128 MiB of HBM per device.

```python
import math
import jax
import jax.numpy as jnp
from jax import lax

DMAX = 2048
K = 256
ROWS_DEV = 1024
VIEWS = 12
ROWS = 32768
RB = 64
N_SENT = 32


def draw_sketched(key, part):
    first, second = jax.random.split(key, 2)
    values = jnp.clip(jax.random.normal(first, (VIEWS, ROWS, DMAX), jnp.float32), -6.0, 6.0)
    blocks = ROWS // ROWS_DEV
    block_pos = (jnp.arange(ROWS) // ROWS_DEV).astype(jnp.float32)
    rising = jnp.exp(jnp.log(4.0) * block_pos / max(blocks - 1, 1))
    rough = jax.random.uniform(second, (VIEWS, ROWS, 1), jnp.float32, 0.7, 1.4)
    return (values * rough * rising[None, :, None]).astype(jnp.bfloat16)


def draw_widths(key, part):
    step = DMAX // 16
    first, second, third = jax.random.split(key, 3)
    base = jax.random.randint(first, (VIEWS,), 2, 17) * step
    top = jax.random.randint(second, (), 0, VIEWS)
    low = (top + 1 + jax.random.randint(third, (), 0, VIEWS - 1)) % VIEWS
    return base.at[top].set(DMAX).at[low].set(2 * step).astype(jnp.int32)


def draw_inv_factor(key, part):
    first, second = jax.random.split(key, 2)
    diag = jax.random.uniform(first, (VIEWS, DMAX, 1), jnp.float32, 1.0, 2.0)
    off = jax.random.normal(second, (VIEWS, DMAX, DMAX), jnp.float32)
    rowpos = jnp.arange(DMAX)[:, None]
    colpos = jnp.arange(DMAX)[None, :]
    rowscale = 0.5 / jnp.sqrt(rowpos.astype(jnp.float32) + 1.0)
    lower_part = jnp.where(colpos < rowpos, off * rowscale[None], 0.0)
    diagonal = jnp.where(colpos == rowpos, 1.0, 0.0)[None] * diag
    return (lower_part + diagonal).astype(jnp.float32)


def levels(own_key, extent, pieces, low, largest):
    factor_of = 1.0
    for axis_at, parts in pieces:
        steps = jax.random.uniform(jax.random.fold_in(jax.random.fold_in(own_key, 6), axis_at), (parts,), jnp.float32, low / len(pieces), largest / len(pieces))
        factor_of = factor_of * jnp.repeat(jnp.exp(steps), extent[axis_at] // parts).reshape((-1,) + (1,) * (len(extent) - 1 - axis_at))
    return factor_of


def noise(rng, shape, scale, bound, shards=(), held_as=jnp.bfloat16):
    entries = scale * jax.random.normal(rng, shape, jnp.float32)
    if shards:
        entries = entries * levels(rng, shape, shards, -0.22, 0.18)
    return jnp.clip(entries, -bound, bound).astype(held_as)


def setup_inputs(seed: int = 0) -> dict:
    seeds = jax.random.split(jax.random.key(seed), 5)
    return {
        "sketched": draw_sketched(jax.random.fold_in(seeds[4], 71), 0),
        "widths": draw_widths(jax.random.fold_in(seeds[4], 71), 0),
        "inv_factor": draw_inv_factor(jax.random.fold_in(seeds[4], 71), 0),
        "shared": noise(seeds[3], (ROWS, K), 1.0, 6.0, ((0, 32),)),
    }


def reference(sketched, widths, inv_factor, shared):
    scale = 1.0 / math.sqrt(ROWS)
    shared_f = shared.astype(jnp.float32).reshape(N_SENT, ROWS_DEV, K)
    high = lax.Precision.HIGHEST

    def one_view(args):
        feats, width, inverse = args
        keep = (jnp.arange(DMAX) < width).astype(jnp.float32)[:, None]
        blocks = feats.astype(jnp.float32).reshape(N_SENT, ROWS_DEV, DMAX)
        terms = jnp.einsum('srd,srk->sdk', blocks, shared_f) * scale
        proj = lax.optimization_barrier(jnp.sum(terms, axis=0)) * keep
        half = jnp.dot(inverse, proj, precision=high) * keep
        back = jnp.einsum('sid,sik->sdk', inverse.reshape(N_SENT, RB, DMAX), half.reshape(N_SENT, RB, K), precision=high)
        load = lax.optimization_barrier(jnp.sum(back, axis=0)) * keep
        contrib = jnp.dot(feats.astype(jnp.float32), load.astype(jnp.bfloat16).astype(jnp.float32), preferred_element_type=jnp.float32)
        return (load, contrib)
    loadings, contribs = lax.map(one_view, (sketched, widths, inv_factor))
    merged = lax.optimization_barrier(jnp.sum(contribs, axis=0))
    gram = lax.dot_general(merged, merged, (((0,), (0,)), ((), ())), precision=high)
    lower = jnp.linalg.cholesky(gram)
    updated = lax.linalg.triangular_solve(lower, merged, left_side=False, lower=True, transpose_a=True) * math.sqrt(ROWS)
    return (loadings, updated)
```

```python
import math

import jax
import jax.numpy as jnp
from jax import lax
from jax.experimental import pallas as pl
from jax.experimental.pallas import tpu as pltpu
from jax.sharding import PartitionSpec as P

MESH = pl.DeviceIdType.MESH
HIGH = lax.Precision.HIGHEST
F32 = jnp.float32
BF16 = jnp.bfloat16
NX, NZ, NY = 4, 8, 4
SEMS = 256


class Links:
    def __init__(self, send_sems, recv_sems):
        self.send_sems, self.recv_sems, self.used, self.sent = send_sems, recv_sems, 0, []

    def slot(self):
        self.used += 1
        assert self.used <= SEMS
        return self.used - 1

    def copy(self, slot, src, dst, device):
        return pltpu.make_async_remote_copy(
            src_ref=src, dst_ref=dst, send_sem=self.send_sems.at[slot], recv_sem=self.recv_sems.at[slot],
            device_id=device, device_id_type=MESH)

    def send(self, slot, src, dst, device):
        made = self.copy(slot, src, dst, device)
        made.start()
        self.sent.append(made)

    def arrived(self, slot, dst, device):
        self.copy(slot, dst, dst, device).wait_recv()

    def drain(self):
        for made in self.sent:
            made.wait_send()
        self.sent = []


class Ring:
    def __init__(self, links, size, pos, device):
        self.links, self.size, self.pos, self.device = links, size, pos, device

    def at(self, delta):
        return lax.rem(self.pos + (delta % self.size), self.size)


class ReduceScatter:
    def __init__(self, ring, own, landing):
        self.ring, self.own, self.landing = ring, own, landing
        self.half_ring = ring.size // 2
        self.slots = {(d, kind, t): ring.links.slot()
                      for t in range(1, self.half_ring + 1) for d in (0, 1) for kind in (0, 1)
                      if not (kind == 1 and t == self.half_ring)}

    def wait(self, d, kind, t):
        sign = (-1, 1)[d]
        buf = self.landing.at[d, kind, t - 1]
        self.ring.links.arrived(self.slots[d, kind, t], buf, self.ring.device(sign))
        return buf

    def step(self, t):
        for kind in (0, 1):
            for d, sign in ((0, -1), (1, 1)):
                if (d, kind, t) not in self.slots:
                    continue
                dist = self.half_ring + 1 - t - kind
                mine = self.own(self.ring.at(sign * dist), d if kind == 0 else 1 - d)
                if t == 1:
                    src = mine
                else:
                    src = self.wait(d, kind, t - 1)
                    src[...] = src[...] + mine[...]
                self.ring.links.send(self.slots[d, kind, t], src, self.landing.at[d, kind, t - 1],
                                     self.ring.device(sign))

    def final(self):
        last = self.half_ring
        out = []
        for h in (0, 1):
            far = self.wait(h, 0, last)
            near = self.wait(1 - h, 1, last - 1)
            out.append(self.own(self.ring.pos, h)[...] + far[...] + near[...])
        return out


class AllGather:
    def __init__(self, ring, full, half):
        self.ring, self.full, self.half = ring, full, half
        self.half_ring = ring.size // 2
        self.slots = {(d, t): ring.links.slot() for t in range(1, self.half_ring + 1) for d in (0, 1)}

    def view(self, d, t, owner):
        return self.half(owner, d) if t == self.half_ring else self.full(owner)

    def wait(self, d, t):
        sign = (-1, 1)[d]
        dst = self.view(d, t, self.ring.at(-sign * t))
        self.ring.links.arrived(self.slots[d, t], dst, self.ring.device(sign))

    def step(self, t):
        for d, sign in ((0, -1), (1, 1)):
            if t > 1:
                self.wait(d, t - 1)
            src = self.view(d, t, self.ring.at(-sign * (t - 1)))
            self.ring.links.send(self.slots[d, t], src, src, self.ring.device(sign))

    def final(self):
        for d in (0, 1):
            self.wait(d, self.half_ring)


def place():
    y, s, c = lax.axis_index("view"), lax.axis_index("sent"), lax.axis_index("col")
    return y, s // NZ, lax.rem(s, NZ), c


def rings(links, x, z, y):
    def x_dev(sign):
        return {"sent": lax.rem(x + (sign % NX), NX) * NZ + z}

    def z_dev(sign):
        return {"sent": x * NZ + lax.rem(z + (sign % NZ), NZ)}

    def y_dev(sign):
        return {"view": lax.rem(y + (sign % NY), NY)}

    return Ring(links, NX, x, x_dev), Ring(links, NZ, z, z_dev), Ring(links, NY, y, y_dev)


def greet(devices):
    barrier = pltpu.get_barrier_semaphore()
    for device in devices:
        pl.semaphore_signal(barrier, inc=1, device_id=device, device_id_type=MESH)
    pl.semaphore_wait(barrier, len(devices))


def nt(a, b):
    return lax.dot_general(a, b, (((1,), (1,)), ((), ())), precision=HIGH, preferred_element_type=F32)


def nn(a, b):
    return lax.dot_general(a, b, (((1,), (0,)), ((), ())), precision=HIGH, preferred_element_type=F32)


def project(scale, widths, shared, inv, sketched, loadings, contrib,
            feats, sharedT, terms, land_x, quarter, land_z, land_z2, quarter2, land_x2, proj, invx,
            part, part_in, part_sum, land_h, half, back, land_b, loadT, stage,
            send_sems, recv_sems, feat_sems, out_sems, own_sem):
    y, x, z, c = place()
    links = Links(send_sems, recv_sems)
    rx, rz, _ = rings(links, x, z, y)
    partner = {"col": 1 - c}
    across = {"sent": lax.rem(x + 2, NX) * NZ + z}

    quarters = [lax.rem(x + d, NX) for d in (2, 3, 1, 0)]
    loads = {}
    for i, v in enumerate((2, 0, 1)):
        for n, q in enumerate(quarters):
            loads[v, n] = pltpu.make_async_copy(
                sketched.at[v, :, pl.ds(pl.multiple_of(q * 256, 256), 256)], feats.at[v, q],
                feat_sems.at[4 * i + n])
            loads[v, n].start()
    own_inv = pltpu.make_async_copy(
        inv.at[:, :, pl.ds(pl.multiple_of(x * 256, 256), 256)], invx.at[:, x], own_sem)
    own_inv.start()
    sharedT[...] = shared[...].T

    greet([rx.device(-1), rx.device(1), rz.device(-1), rz.device(1), across, partner])

    def make_terms(v):
        for n, q in enumerate(quarters):
            loads[v, n].wait()
            terms[v, q] = jnp.dot(sharedT[...], feats[v, q], preferred_element_type=F32).reshape(NZ, 32, 256)

    xs = [ReduceScatter(rx, lambda o, h, v=v: terms.at[v, o, pl.ds(4 * h, 4)], land_x.at[v]) for v in (0, 1)]
    zs = [ReduceScatter(rz, lambda o, h, v=v: quarter.at[v, o, pl.ds(16 * h, 16)], land_z.at[v]) for v in (0, 1)]
    z2 = ReduceScatter(rz, lambda o, h: terms.at[2, :, o, pl.ds(16 * h, 16)], land_z2)
    x2 = ReduceScatter(rx, lambda o, h: quarter2.at[o, pl.ds(16 * h, 16)], land_x2)

    def lanes_kept(v, first, value):
        col = first + lax.broadcasted_iota(jnp.int32, value.shape, 1)
        return jnp.where(col < widths[v], value, 0.0)

    first_col = c * 1024 + x * 256

    def own_proj(v, halves):
        for h in (0, 1):
            proj[z, v, pl.ds(16 * h, 16)] = lanes_kept(v, first_col, halves[h] * scale)

    def own_quarter(v):
        halves = xs[v].final()
        for h in (0, 1):
            quarter[v, pl.ds(4 * h, 4)] = halves[h]

    make_terms(2)
    z2.step(1)
    make_terms(0)
    xs[0].step(1)
    make_terms(1)
    xs[1].step(1)
    z2.step(2)
    xs[0].step(2)
    z2.step(3)
    xs[1].step(2)
    own_quarter(0)
    zs[0].step(1)
    z2.step(4)
    zs[0].step(2)
    own_quarter(1)
    zs[1].step(1)
    halves = z2.final()
    for h in (0, 1):
        quarter2[:, pl.ds(16 * h, 16)] = halves[h]
    x2.step(1)
    zs[0].step(3)
    zs[1].step(2)
    x2.step(2)
    inv_slots = {d: links.slot() for d in (1, 3, 2)}
    inv_dev = {1: rx.device(1), 3: rx.device(-1), 2: across}
    for d in (1, 3, 2):
        q = rx.at(d)
        links.send(inv_slots[d], inv.at[:, :, pl.ds(pl.multiple_of(q * 256, 256), 256)], invx.at[:, x], inv_dev[d])
    zs[0].step(4)
    zs[1].step(3)
    own_proj(2, x2.final())
    own_proj(0, zs[0].final())
    zs[1].step(4)
    own_proj(1, zs[1].final())

    gather = AllGather(rz, lambda o: proj.at[o], lambda o, h: proj.at[o, :, pl.ds(16 * h, 16)])
    for t in range(1, 5):
        gather.step(t)
    own_inv.wait()
    for d in (1, 3, 2):
        links.arrived(inv_slots[d], invx.at[:, rx.at(-d)], inv_dev[d])
    gather.final()

    for v in range(3):
        product = nt(proj[:, v].reshape(256, 256), invx[v].reshape(256, 256)).reshape(2, NX, 32, 256)
        part[:, :, v] = product
    slot = links.slot()
    links.send(slot, part.at[1 - c], part_in, partner)
    links.arrived(slot, part_in, partner)
    part_sum[...] = part[c] + part_in[...]
    hs = ReduceScatter(rx, lambda o, h: part_sum.at[o, :, pl.ds(16 * h, 16)], land_h)
    hs.step(1)
    hs.step(2)
    halves = hs.final()
    lane = lax.broadcasted_iota(jnp.int32, (16, 256), 1)
    row = (lane // 64) * (64 * NZ) + z * 64 + lax.rem(lane, 64)
    for h in (0, 1):
        for v in range(3):
            half[c, x, v, pl.ds(16 * h, 16)] = jnp.where(row < widths[v], halves[h][v], 0.0)
    hg = AllGather(rx, lambda o: half.at[c, o], lambda o, h: half.at[c, o, :, pl.ds(16 * h, 16)])
    hg.step(1)
    hg.step(2)
    hg.final()
    slot = links.slot()
    links.send(slot, half.at[c], half.at[c], partner)
    links.arrived(slot, half.at[1 - c], partner)

    for v in range(3):
        back[:, v] = nn(half[:, :, v].reshape(256, 256), invx[v].reshape(256, 256)).reshape(NZ, 32, 256)
    bs = ReduceScatter(rz, lambda o, h: back.at[o, :, pl.ds(16 * h, 16)], land_b)
    for t in range(1, 5):
        bs.step(t)
    halves = bs.final()
    for h in (0, 1):
        for v in range(3):
            loadT[v, x, z, pl.ds(16 * h, 16)] = lanes_kept(v, first_col, halves[h][v])

    gz = AllGather(rz, lambda o: loadT.at[pl.ds(0, 2), x, o], lambda o, h: loadT.at[pl.ds(0, 2), x, o, pl.ds(16 * h, 16)])
    gx = AllGather(rx, lambda o: loadT.at[pl.ds(0, 2), o], lambda o, h: loadT.at[pl.ds(0, 2), o, pl.ds(4 * h, 4)])
    g2x = AllGather(rx, lambda o: loadT.at[2, o, z], lambda o, h: loadT.at[2, o, z, pl.ds(16 * h, 16)])
    g2z = AllGather(rz, lambda o: loadT.at[2, :, o], lambda o, h: loadT.at[2, :, o, pl.ds(16 * h, 16)])

    outs = []

    def use(v, q, first=False):
        block = loadT[v, q].reshape(256, 256).T
        stage[v, q] = block
        out = pltpu.make_async_copy(
            stage.at[v, q], loadings.at[v, pl.ds(pl.multiple_of(q * 256, 256), 256)], out_sems.at[len(outs)])
        out.start()
        outs.append(out)
        product = jnp.dot(feats[v, q], block.astype(BF16), preferred_element_type=F32)
        contrib[...] = product if first else contrib[...] + product

    g2x.step(1)
    gz.step(1)
    g2x.step(2)
    gz.step(2)
    g2x.final()
    g2z.step(1)
    gz.step(3)
    gz.step(4)
    gz.final()
    gx.step(1)
    g2z.step(2)
    use(0, x, True)
    use(1, x)
    g2z.step(3)
    gx.step(2)
    g2z.step(4)
    for d in (1, 3):
        for v in (0, 1):
            use(v, rx.at(d))
    g2z.final()
    for d in range(4):
        use(2, rx.at(d))
    gx.final()
    for v in (0, 1):
        use(v, rx.at(2))
    links.drain()
    for out in outs:
        out.wait()


def merge(contrib, merged, gram, mine_in, mine_sum, land_m, part, part_in, part_sum, land_g, over_x, over_z, total,
          send_sems, recv_sems):
    y, x, z, c = place()
    links = Links(send_sems, recv_sems)
    rx, rz, ry = rings(links, x, z, y)
    partner = {"col": 1 - c}
    greet([rx.device(-1), rx.device(1), rz.device(-1), rz.device(1), ry.device(-1), ry.device(1), partner])

    slot = links.slot()
    links.send(slot, contrib.at[1 - c], mine_in, partner)
    links.arrived(slot, mine_in, partner)
    mine_sum[...] = contrib[c] + mine_in[...]
    ms = ReduceScatter(ry, lambda o, h: mine_sum.at[o, pl.ds(64 * h, 64)], land_m)
    ms.step(1)
    ms.step(2)
    halves = ms.final()
    for h in (0, 1):
        merged[c, y, pl.ds(64 * h, 64)] = halves[h]
    rows = merged[c, y]
    part[...] = lax.dot_general(rows, rows, (((0,), (0,)), ((), ())), precision=HIGH,
                                preferred_element_type=F32).reshape(2, NY, 32, 256)
    slot = links.slot()
    links.send(slot, part.at[1 - c], part_in, partner)
    mg = AllGather(ry, lambda o: merged.at[c, o], lambda o, h: merged.at[c, o, pl.ds(64 * h, 64)])
    links.arrived(slot, part_in, partner)
    part_sum[...] = part[c] + part_in[...]
    gs = ReduceScatter(ry, lambda o, h: part_sum.at[o, pl.ds(16 * h, 16)], land_g)
    gs.step(1)
    gs.step(2)
    halves = gs.final()
    for h in (0, 1):
        over_x[x, pl.ds(16 * h, 16)] = halves[h]
    gx = AllGather(rx, lambda o: over_x.at[o], lambda o, h: over_x.at[o, pl.ds(16 * h, 16)])
    gx.step(1)
    mg.step(1)
    gx.step(2)
    gx.final()
    over_z[z] = (over_x[0] + over_x[1]) + (over_x[2] + over_x[3])
    gz = AllGather(rz, lambda o: over_z.at[o], lambda o, h: over_z.at[o, pl.ds(16 * h, 16)])
    gz.step(1)
    mg.step(2)
    gz.step(2)
    mg.final()
    slot = links.slot()
    links.send(slot, merged.at[c], merged.at[c], partner)
    gz.step(3)
    gz.step(4)
    gz.final()
    acc = over_z[0]
    for i in range(1, NZ):
        acc = acc + over_z[i]
    gram[c, y] = acc
    gy = AllGather(ry, lambda o: gram.at[c, o], lambda o, h: gram.at[c, o, pl.ds(16 * h, 16)])
    gy.step(1)
    gy.step(2)
    gy.final()
    last = links.slot()
    links.send(last, gram.at[c], gram.at[c], partner)
    links.arrived(slot, merged.at[1 - c], partner)
    links.arrived(last, gram.at[1 - c], partner)
    links.drain()


def shards(sketched, widths, inv_factor, shared):
    total_rows = shared.shape[0] * lax.axis_size("sent")
    vmem, smem, anywhere = (pl.BlockSpec(memory_space=m) for m in (pltpu.VMEM, pltpu.SMEM, pl.ANY))

    def buf(*shape):
        return pltpu.VMEM(shape, F32)

    sems = [pltpu.SemaphoreType.DMA((SEMS,)), pltpu.SemaphoreType.DMA((SEMS,))]

    def kernel_a(*refs):
        project(1.0 / math.sqrt(total_rows), *refs)

    loadings, contrib = pl.pallas_call(
        kernel_a,
        name="project",
        out_shape=(jax.ShapeDtypeStruct((3, 1024, 256), F32), jax.ShapeDtypeStruct((1024, 256), F32)),
        in_specs=[smem, vmem, vmem, anywhere],
        out_specs=(anywhere, vmem),
        scratch_shapes=[
            pltpu.VMEM((3, 4, 1024, 256), BF16), pltpu.VMEM((256, 1024), BF16),
            buf(3, 4, 8, 32, 256), buf(2, 2, 2, 2, 4, 32, 256), buf(2, 8, 32, 256), buf(2, 2, 2, 4, 16, 256),
            buf(2, 2, 4, 4, 16, 256), buf(4, 32, 256), buf(2, 2, 2, 16, 256), buf(8, 3, 32, 256),
            buf(3, 4, 64, 256), buf(2, 4, 3, 32, 256), buf(4, 3, 32, 256), buf(4, 3, 32, 256),
            buf(2, 2, 2, 3, 16, 256), buf(2, 4, 3, 32, 256), buf(8, 3, 32, 256), buf(2, 2, 4, 3, 16, 256),
            buf(3, 4, 8, 32, 256), buf(3, 4, 256, 256), *sems,
            pltpu.SemaphoreType.DMA((12,)), pltpu.SemaphoreType.DMA((12,)), pltpu.SemaphoreType.DMA],
        compiler_params=pltpu.CompilerParams(collective_id=0, has_side_effects=True, vmem_limit_bytes=56 * 2**20),
    )(widths, shared, inv_factor, sketched)

    merged, gram = pl.pallas_call(
        merge,
        name="merge",
        out_shape=(jax.ShapeDtypeStruct((2, NY, 128, 256), F32), jax.ShapeDtypeStruct((2, NY, 32, 256), F32)),
        in_specs=[vmem],
        out_specs=(vmem, vmem),
        scratch_shapes=[
            buf(4, 128, 256), buf(4, 128, 256), buf(2, 2, 2, 64, 256), buf(2, 4, 32, 256), buf(4, 32, 256),
            buf(4, 32, 256), buf(2, 2, 2, 16, 256), buf(4, 32, 256), buf(8, 32, 256), buf(2, 4, 32, 256), *sems],
        compiler_params=pltpu.CompilerParams(collective_id=1, has_side_effects=True, vmem_limit_bytes=32 * 2**20),
    )(contrib.reshape(2, NY, 128, 256))
    merged, gram = merged.reshape(1024, 256), gram.reshape(256, 256)
    lower = jnp.linalg.cholesky(gram)
    updated = lax.linalg.triangular_solve(
        lower, merged, left_side=False, lower=True, transpose_a=True
    ) * math.sqrt(total_rows)
    return (loadings, updated)


def solution(mesh):
    return jax.shard_map(
        shards,
        mesh=mesh,
        in_specs=(P("view", "sent", "col"), P("view"), P("view", "sent", "col"), P("sent", None)),
        out_specs=(P("view", "col", None), P("sent", None)),
        check_vma=False,
    )
```

```python
import math

import jax
import jax.numpy as jnp
from jax import lax
from jax.experimental import pallas as pl
from jax.experimental.pallas import tpu as pltpu
from jax.sharding import PartitionSpec as P

MESH = pl.DeviceIdType.MESH
HIGH = lax.Precision.HIGHEST
F32 = jnp.float32
BF16 = jnp.bfloat16
NX, NZ, NY = 4, 8, 4
SEMS = 256


class Links:
    def __init__(self, send_sems, recv_sems):
        self.send_sems, self.recv_sems, self.used, self.sent = send_sems, recv_sems, 0, []

    def slot(self):
        self.used += 1
        assert self.used <= SEMS
        return self.used - 1

    def copy(self, slot, src, dst, device):
        return pltpu.make_async_remote_copy(
            src_ref=src, dst_ref=dst, send_sem=self.send_sems.at[slot], recv_sem=self.recv_sems.at[slot],
            device_id=device, device_id_type=MESH)

    def send(self, slot, src, dst, device):
        made = self.copy(slot, src, dst, device)
        made.start()
        self.sent.append(made)

    def arrived(self, slot, dst, device):
        self.copy(slot, dst, dst, device).wait_recv()

    def drain(self):
        for made in self.sent:
            made.wait_send()
        self.sent = []


class Ring:
    def __init__(self, links, size, pos, device):
        self.links, self.size, self.pos, self.device = links, size, pos, device

    def at(self, delta):
        return lax.rem(self.pos + (delta % self.size), self.size)


class ReduceScatter:
    def __init__(self, ring, own, landing):
        self.ring, self.own, self.landing = ring, own, landing
        self.half_ring = ring.size // 2
        self.slots = {(d, kind, t): ring.links.slot()
                      for t in range(1, self.half_ring + 1) for d in (0, 1) for kind in (0, 1)
                      if not (kind == 1 and t == self.half_ring)}

    def wait(self, d, kind, t):
        sign = (-1, 1)[d]
        buf = self.landing.at[d, kind, t - 1]
        self.ring.links.arrived(self.slots[d, kind, t], buf, self.ring.device(sign))
        return buf

    def step(self, t):
        for kind in (0, 1):
            for d, sign in ((0, -1), (1, 1)):
                if (d, kind, t) not in self.slots:
                    continue
                dist = self.half_ring + 1 - t - kind
                mine = self.own(self.ring.at(sign * dist), d if kind == 0 else 1 - d)
                if t == 1:
                    src = mine
                else:
                    src = self.wait(d, kind, t - 1)
                    src[...] = src[...] + mine[...]
                self.ring.links.send(self.slots[d, kind, t], src, self.landing.at[d, kind, t - 1],
                                     self.ring.device(sign))

    def final(self):
        last = self.half_ring
        out = []
        for h in (0, 1):
            far = self.wait(h, 0, last)
            near = self.wait(1 - h, 1, last - 1)
            out.append(self.own(self.ring.pos, h)[...] + far[...] + near[...])
        return out


class AllGather:
    def __init__(self, ring, full, half):
        self.ring, self.full, self.half = ring, full, half
        self.half_ring = ring.size // 2
        self.slots = {(d, t): ring.links.slot() for t in range(1, self.half_ring + 1) for d in (0, 1)}

    def view(self, d, t, owner):
        return self.half(owner, d) if t == self.half_ring else self.full(owner)

    def wait(self, d, t):
        sign = (-1, 1)[d]
        dst = self.view(d, t, self.ring.at(-sign * t))
        self.ring.links.arrived(self.slots[d, t], dst, self.ring.device(sign))

    def step(self, t):
        for d, sign in ((0, -1), (1, 1)):
            if t > 1:
                self.wait(d, t - 1)
            src = self.view(d, t, self.ring.at(-sign * (t - 1)))
            self.ring.links.send(self.slots[d, t], src, src, self.ring.device(sign))

    def final(self):
        for d in (0, 1):
            self.wait(d, self.half_ring)


def place():
    y, s, c = lax.axis_index("view"), lax.axis_index("sent"), lax.axis_index("col")
    return y, s // NZ, lax.rem(s, NZ), c


def rings(links, x, z, y):
    def x_dev(sign):
        return {"sent": lax.rem(x + (sign % NX), NX) * NZ + z}

    def z_dev(sign):
        return {"sent": x * NZ + lax.rem(z + (sign % NZ), NZ)}

    def y_dev(sign):
        return {"view": lax.rem(y + (sign % NY), NY)}

    return Ring(links, NX, x, x_dev), Ring(links, NZ, z, z_dev), Ring(links, NY, y, y_dev)


def greet(devices):
    barrier = pltpu.get_barrier_semaphore()
    for device in devices:
        pl.semaphore_signal(barrier, inc=1, device_id=device, device_id_type=MESH)
    pl.semaphore_wait(barrier, len(devices))


def nt(a, b):
    return lax.dot_general(a, b, (((1,), (1,)), ((), ())), precision=HIGH, preferred_element_type=F32)


def nn(a, b):
    return lax.dot_general(a, b, (((1,), (0,)), ((), ())), precision=HIGH, preferred_element_type=F32)


def project(scale, widths, shared, inv, sketched, loadings, contrib,
            feats, sharedT, terms, land_x, quarter, land_z, land_z2, quarter2, land_x2, proj, invx,
            part, part_in, part_sum, land_h, half, back, land_b, loadT, stage,
            send_sems, recv_sems, feat_sems, out_sems, own_sem):
    y, x, z, c = place()
    links = Links(send_sems, recv_sems)
    rx, rz, _ = rings(links, x, z, y)
    partner = {"col": 1 - c}
    across = {"sent": lax.rem(x + 2, NX) * NZ + z}

    quarters = [lax.rem(x + d, NX) for d in (2, 3, 1, 0)]
    loads = {}
    for i, v in enumerate((2, 0, 1)):
        for n, q in enumerate(quarters):
            loads[v, n] = pltpu.make_async_copy(
                sketched.at[v, :, pl.ds(pl.multiple_of(q * 256, 256), 256)], feats.at[v, q],
                feat_sems.at[4 * i + n])
            loads[v, n].start()
    own_inv = pltpu.make_async_copy(
        inv.at[:, :, pl.ds(pl.multiple_of(x * 256, 256), 256)], invx.at[:, x], own_sem)
    own_inv.start()
    sharedT[...] = shared[...].T

    greet([rx.device(-1), rx.device(1), rz.device(-1), rz.device(1), across, partner])

    def make_terms(v):
        for n, q in enumerate(quarters):
            loads[v, n].wait()
            terms[v, q] = jnp.dot(sharedT[...], feats[v, q], preferred_element_type=F32).reshape(NZ, 32, 256)

    xs = [ReduceScatter(rx, lambda o, h, v=v: terms.at[v, o, pl.ds(4 * h, 4)], land_x.at[v]) for v in (0, 1)]
    zs = [ReduceScatter(rz, lambda o, h, v=v: quarter.at[v, o, pl.ds(16 * h, 16)], land_z.at[v]) for v in (0, 1)]
    z2 = ReduceScatter(rz, lambda o, h: terms.at[2, :, o, pl.ds(16 * h, 16)], land_z2)
    x2 = ReduceScatter(rx, lambda o, h: quarter2.at[o, pl.ds(16 * h, 16)], land_x2)

    def lanes_kept(v, first, value):
        col = first + lax.broadcasted_iota(jnp.int32, value.shape, 1)
        return jnp.where(col < widths[v], value, 0.0)

    first_col = c * 1024 + x * 256

    def own_proj(v, halves):
        for h in (0, 1):
            proj[z, v, pl.ds(16 * h, 16)] = lanes_kept(v, first_col, halves[h] * scale)

    def own_quarter(v):
        halves = xs[v].final()
        for h in (0, 1):
            quarter[v, pl.ds(4 * h, 4)] = halves[h]

    make_terms(2)
    z2.step(1)
    make_terms(0)
    xs[0].step(1)
    make_terms(1)
    xs[1].step(1)
    z2.step(2)
    xs[0].step(2)
    z2.step(3)
    xs[1].step(2)
    own_quarter(0)
    zs[0].step(1)
    z2.step(4)
    zs[0].step(2)
    own_quarter(1)
    zs[1].step(1)
    halves = z2.final()
    for h in (0, 1):
        quarter2[:, pl.ds(16 * h, 16)] = halves[h]
    x2.step(1)
    zs[0].step(3)
    zs[1].step(2)
    x2.step(2)
    inv_slots = {d: links.slot() for d in (1, 3, 2)}
    inv_dev = {1: rx.device(1), 3: rx.device(-1), 2: across}
    for d in (1, 3, 2):
        q = rx.at(d)
        links.send(inv_slots[d], inv.at[:, :, pl.ds(pl.multiple_of(q * 256, 256), 256)], invx.at[:, x], inv_dev[d])
    zs[0].step(4)
    zs[1].step(3)
    own_proj(2, x2.final())
    own_proj(0, zs[0].final())
    zs[1].step(4)
    own_proj(1, zs[1].final())

    gather = AllGather(rz, lambda o: proj.at[o], lambda o, h: proj.at[o, :, pl.ds(16 * h, 16)])
    for t in range(1, 5):
        gather.step(t)
    own_inv.wait()
    for d in (1, 3, 2):
        links.arrived(inv_slots[d], invx.at[:, rx.at(-d)], inv_dev[d])
    gather.final()

    for v in range(3):
        product = nt(proj[:, v].reshape(256, 256), invx[v].reshape(256, 256)).reshape(2, NX, 32, 256)
        part[:, :, v] = product
    slot = links.slot()
    links.send(slot, part.at[1 - c], part_in, partner)
    links.arrived(slot, part_in, partner)
    part_sum[...] = part[c] + part_in[...]
    hs = ReduceScatter(rx, lambda o, h: part_sum.at[o, :, pl.ds(16 * h, 16)], land_h)
    hs.step(1)
    hs.step(2)
    halves = hs.final()
    lane = lax.broadcasted_iota(jnp.int32, (16, 256), 1)
    row = (lane // 64) * (64 * NZ) + z * 64 + lax.rem(lane, 64)
    for h in (0, 1):
        for v in range(3):
            half[c, x, v, pl.ds(16 * h, 16)] = jnp.where(row < widths[v], halves[h][v], 0.0)
    hg = AllGather(rx, lambda o: half.at[c, o], lambda o, h: half.at[c, o, :, pl.ds(16 * h, 16)])
    hg.step(1)
    hg.step(2)
    hg.final()
    slot = links.slot()
    links.send(slot, half.at[c], half.at[c], partner)
    links.arrived(slot, half.at[1 - c], partner)

    for v in range(3):
        back[:, v] = nn(half[:, :, v].reshape(256, 256), invx[v].reshape(256, 256)).reshape(NZ, 32, 256)
    bs = ReduceScatter(rz, lambda o, h: back.at[o, :, pl.ds(16 * h, 16)], land_b)
    for t in range(1, 5):
        bs.step(t)
    halves = bs.final()
    for h in (0, 1):
        for v in range(3):
            loadT[v, x, z, pl.ds(16 * h, 16)] = lanes_kept(v, first_col, halves[h][v])

    gz = AllGather(rz, lambda o: loadT.at[pl.ds(0, 2), x, o], lambda o, h: loadT.at[pl.ds(0, 2), x, o, pl.ds(16 * h, 16)])
    gx = AllGather(rx, lambda o: loadT.at[pl.ds(0, 2), o], lambda o, h: loadT.at[pl.ds(0, 2), o, pl.ds(4 * h, 4)])
    g2x = AllGather(rx, lambda o: loadT.at[2, o, z], lambda o, h: loadT.at[2, o, z, pl.ds(16 * h, 16)])
    g2z = AllGather(rz, lambda o: loadT.at[2, :, o], lambda o, h: loadT.at[2, :, o, pl.ds(16 * h, 16)])

    outs = []

    def use(v, q, first=False):
        block = loadT[v, q].reshape(256, 256).T
        stage[v, q] = block
        out = pltpu.make_async_copy(
            stage.at[v, q], loadings.at[v, pl.ds(pl.multiple_of(q * 256, 256), 256)], out_sems.at[len(outs)])
        out.start()
        outs.append(out)
        product = jnp.dot(feats[v, q], block.astype(BF16), preferred_element_type=F32)
        contrib[...] = product if first else contrib[...] + product

    g2x.step(1)
    gz.step(1)
    g2x.step(2)
    gz.step(2)
    g2x.final()
    g2z.step(1)
    gz.step(3)
    gz.step(4)
    gz.final()
    gx.step(1)
    g2z.step(2)
    use(0, x, True)
    use(1, x)
    g2z.step(3)
    gx.step(2)
    g2z.step(4)
    for d in (1, 3):
        for v in (0, 1):
            use(v, rx.at(d))
    g2z.final()
    for d in range(4):
        use(2, rx.at(d))
    gx.final()
    for v in (0, 1):
        use(v, rx.at(2))
    links.drain()
    for out in outs:
        out.wait()


def merge(contrib, merged, gram, mine_in, mine_sum, land_m, part, part_in, part_sum, land_g, over_x, over_z, total,
          send_sems, recv_sems):
    y, x, z, c = place()
    links = Links(send_sems, recv_sems)
    rx, rz, ry = rings(links, x, z, y)
    partner = {"col": 1 - c}
    greet([rx.device(-1), rx.device(1), rz.device(-1), rz.device(1), ry.device(-1), ry.device(1), partner])

    slot = links.slot()
    links.send(slot, contrib.at[1 - c], mine_in, partner)
    links.arrived(slot, mine_in, partner)
    mine_sum[...] = contrib[c] + mine_in[...]
    ms = ReduceScatter(ry, lambda o, h: mine_sum.at[o, pl.ds(64 * h, 64)], land_m)
    ms.step(1)
    ms.step(2)
    halves = ms.final()
    for h in (0, 1):
        merged[c, y, pl.ds(64 * h, 64)] = halves[h]
    rows = merged[c, y]
    part[...] = lax.dot_general(rows, rows, (((0,), (0,)), ((), ())), precision=HIGH,
                                preferred_element_type=F32).reshape(2, NY, 32, 256)
    slot = links.slot()
    links.send(slot, part.at[1 - c], part_in, partner)
    mg = AllGather(ry, lambda o: merged.at[c, o], lambda o, h: merged.at[c, o, pl.ds(64 * h, 64)])
    links.arrived(slot, part_in, partner)
    part_sum[...] = part[c] + part_in[...]
    gs = ReduceScatter(ry, lambda o, h: part_sum.at[o, pl.ds(16 * h, 16)], land_g)
    gs.step(1)
    gs.step(2)
    halves = gs.final()
    for h in (0, 1):
        over_x[x, pl.ds(16 * h, 16)] = halves[h]
    gx = AllGather(rx, lambda o: over_x.at[o], lambda o, h: over_x.at[o, pl.ds(16 * h, 16)])
    gx.step(1)
    mg.step(1)
    gx.step(2)
    gx.final()
    over_z[z] = (over_x[0] + over_x[1]) + (over_x[2] + over_x[3])
    gz = AllGather(rz, lambda o: over_z.at[o], lambda o, h: over_z.at[o, pl.ds(16 * h, 16)])
    gz.step(1)
    mg.step(2)
    gz.step(2)
    mg.final()
    slot = links.slot()
    links.send(slot, merged.at[c], merged.at[c], partner)
    gz.step(3)
    gz.step(4)
    gz.final()
    acc = over_z[0]
    for i in range(1, NZ):
        acc = acc + over_z[i]
    gram[c, y] = acc
    gy = AllGather(ry, lambda o: gram.at[c, o], lambda o, h: gram.at[c, o, pl.ds(16 * h, 16)])
    gy.step(1)
    gy.step(2)
    gy.final()
    last = links.slot()
    links.send(last, gram.at[c], gram.at[c], partner)
    links.arrived(slot, merged.at[1 - c], partner)
    links.arrived(last, gram.at[1 - c], partner)
    links.drain()


PANEL = 32


def panel_inverse(tiles, lane0):
    groups = PANEL // 8
    sub = lax.broadcasted_iota(jnp.int32, (8, 128), 0)
    lane = lax.broadcasted_iota(jnp.int32, (8, 128), 1)

    def spread(tile, s):
        return jnp.broadcast_to(tile[s:s + 1, :], (8, 128))

    cols = [{g: jnp.broadcast_to(tiles[g][:, lane0 + j:lane0 + j + 1], (8, 128)) for g in range(j // 8, groups)}
            for j in range(PANEL)]
    unit = [jnp.where(lane == sub + 8 * g, 1.0, 0.0).astype(F32) for g in range(groups)]
    pivots = [jnp.ones((8, 128), F32) for g in range(groups)]
    for k in range(PANEL):
        gk, sk = divmod(k, 8)
        pivot = spread(cols[k][gk], sk)
        inverse = 1.0 / pivot
        pivots[gk] = jnp.where(sub == sk, pivot, pivots[gk])
        mult = {g: cols[k][g] * inverse for g in range(gk, groups)}
        for j in range(k + 1, PANEL):
            gj, sj = divmod(j, 8)
            entry = spread(cols[k][gj], sj)
            for g in range(gj, groups):
                cols[j][g] = cols[j][g] - mult[g] * entry
        row = spread(unit[gk], sk)
        for g in range(gk, groups):
            m = jnp.where(sub > sk, mult[g], 0.0) if g == gk else mult[g]
            unit[g] = unit[g] - m * row
    return jnp.concatenate([unit[g] * lax.rsqrt(pivots[g]) for g in range(groups)], axis=0)[:, :PANEL]


def tn(a, b):
    return lax.dot_general(a, b, (((0,), (0,)), ((), ())), precision=HIGH, preferred_element_type=F32)


def factor_inverse(work, inverse, between):
    n = work.shape[0]
    for p in range(n // PANEL):
        r0 = p * PANEL
        lt = r0 // 128 * 128
        tiles = [work[r0 + 8 * g:r0 + 8 * g + 8, lt:lt + 128] for g in range(PANEL // 8)]
        block = panel_inverse(tiles, r0 - lt)
        col = lax.broadcasted_iota(jnp.int32, (PANEL, n), 1)
        row = lax.broadcasted_iota(jnp.int32, (PANEL, n), 0)
        here = (col >= r0) & (col < r0 + PANEL)
        wide = jnp.where(here, jnp.where(col == row + r0, 1.0, 0.0), work[r0:r0 + PANEL, :])
        u = nn(block, wide)
        inverse[r0:r0 + PANEL, :] = jnp.where(col < r0 + PANEL, u, 0.0)
        between(p)
        r1 = r0 + PANEL
        if r1 < n:
            base = r1 // 128 * 128
            upd = tn(u[:, base:], u)[r1 - base:]
            col = lax.broadcasted_iota(jnp.int32, (n - r1, n), 1)
            here = (col >= r0) & (col < r1)
            work[r1:, :] = jnp.where(here, 0.0, work[r1:, :]) - upd


def solve(root, gram, merged, loaded, updated, loadings, work, inverse, passing, in_sem, out_sem):
    bring = pltpu.make_async_copy(loaded, passing, in_sem)
    put = pltpu.make_async_copy(passing, loadings, out_sem)
    bring.start()
    work[...] = gram[...]

    def between(panel):
        if panel == 2:
            bring.wait()
            put.start()

    factor_inverse(work, inverse, between)
    updated[...] = nt(merged[...], inverse[...]) * root
    put.wait()


def shards(sketched, widths, inv_factor, shared):
    total_rows = shared.shape[0] * lax.axis_size("sent")
    vmem, smem, anywhere = (pl.BlockSpec(memory_space=m) for m in (pltpu.VMEM, pltpu.SMEM, pl.ANY))

    def buf(*shape):
        return pltpu.VMEM(shape, F32)

    sems = [pltpu.SemaphoreType.DMA((SEMS,)), pltpu.SemaphoreType.DMA((SEMS,))]

    def kernel_a(*refs):
        project(1.0 / math.sqrt(total_rows), *refs)

    loadings, contrib = pl.pallas_call(
        kernel_a,
        name="project",
        out_shape=(jax.ShapeDtypeStruct((3, 1024, 256), F32), jax.ShapeDtypeStruct((1024, 256), F32)),
        in_specs=[smem, vmem, vmem, anywhere],
        out_specs=(anywhere, vmem),
        scratch_shapes=[
            pltpu.VMEM((3, 4, 1024, 256), BF16), pltpu.VMEM((256, 1024), BF16),
            buf(3, 4, 8, 32, 256), buf(2, 2, 2, 2, 4, 32, 256), buf(2, 8, 32, 256), buf(2, 2, 2, 4, 16, 256),
            buf(2, 2, 4, 4, 16, 256), buf(4, 32, 256), buf(2, 2, 2, 16, 256), buf(8, 3, 32, 256),
            buf(3, 4, 64, 256), buf(2, 4, 3, 32, 256), buf(4, 3, 32, 256), buf(4, 3, 32, 256),
            buf(2, 2, 2, 3, 16, 256), buf(2, 4, 3, 32, 256), buf(8, 3, 32, 256), buf(2, 2, 4, 3, 16, 256),
            buf(3, 4, 8, 32, 256), buf(3, 4, 256, 256), *sems,
            pltpu.SemaphoreType.DMA((12,)), pltpu.SemaphoreType.DMA((12,)), pltpu.SemaphoreType.DMA],
        compiler_params=pltpu.CompilerParams(collective_id=0, has_side_effects=True, vmem_limit_bytes=56 * 2**20),
    )(widths, shared, inv_factor, sketched)

    merged, gram = pl.pallas_call(
        merge,
        name="merge",
        out_shape=(jax.ShapeDtypeStruct((2, NY, 128, 256), F32), jax.ShapeDtypeStruct((2, NY, 32, 256), F32)),
        in_specs=[vmem],
        out_specs=(vmem, vmem),
        scratch_shapes=[
            buf(4, 128, 256), buf(4, 128, 256), buf(2, 2, 2, 64, 256), buf(2, 4, 32, 256), buf(4, 32, 256),
            buf(4, 32, 256), buf(2, 2, 2, 16, 256), buf(4, 32, 256), buf(8, 32, 256), buf(2, 4, 32, 256), *sems],
        compiler_params=pltpu.CompilerParams(collective_id=1, has_side_effects=True, vmem_limit_bytes=32 * 2**20),
    )(contrib.reshape(2, NY, 128, 256))
    merged, gram = merged.reshape(1024, 256), gram.reshape(256, 256)

    def kernel_c(*refs):
        solve(math.sqrt(total_rows), *refs)

    updated, loadings = pl.pallas_call(
        kernel_c,
        name="solve",
        out_shape=(jax.ShapeDtypeStruct((1024, 256), F32), jax.ShapeDtypeStruct((3, 1024, 256), F32)),
        in_specs=[vmem, vmem, anywhere],
        out_specs=(vmem, anywhere),
        scratch_shapes=[buf(256, 256), buf(256, 256), buf(3, 1024, 256),
                        pltpu.SemaphoreType.DMA, pltpu.SemaphoreType.DMA],
        compiler_params=pltpu.CompilerParams(vmem_limit_bytes=32 * 2**20),
    )(gram, merged, loadings)
    return (loadings, updated)


def solution(mesh):
    return jax.shard_map(
        shards,
        mesh=mesh,
        in_specs=(P("view", "sent", "col"), P("view"), P("view", "sent", "col"), P("sent", None)),
        out_specs=(P("view", "col", None), P("sent", None)),
        check_vma=False,
    )
```

```python
import math

import jax
import jax.numpy as jnp
from jax import lax
from jax.experimental import pallas as pl
from jax.experimental.pallas import tpu as pltpu
from jax.sharding import PartitionSpec as P

MESH = pl.DeviceIdType.MESH
HIGH = lax.Precision.HIGHEST
F32 = jnp.float32
BF16 = jnp.bfloat16
NX, NZ, NY = 4, 8, 4
SEMS = 256


class Clock:
    def __init__(self):
        self.now, self.busy, self.flows = 0.0, {}, []

    def sent(self, axis, kib):
        rate = 0.0068 if axis == "c" else 0.022
        self.busy[axis] = max(self.now, self.busy.get(axis, 0.0)) + kib * rate
        return self.busy[axis] + (1.0 if axis == "c" else 1.8)

    def add(self, start, flow):
        self.flows.append([start, len(self.flows), flow])

    def run(self):
        while self.flows:
            item = min(self.flows)
            self.now = max(self.now, item[0]) + 0.1
            try:
                item[0] = next(item[2])
            except StopIteration:
                self.flows.remove(item)


class Links:
    def __init__(self, send_sems, recv_sems):
        self.send_sems, self.recv_sems, self.used, self.sent = send_sems, recv_sems, 0, []
        self.clock = Clock()

    def slot(self):
        self.used += 1
        assert self.used <= SEMS
        return self.used - 1

    def copy(self, slot, src, dst, device):
        return pltpu.make_async_remote_copy(
            src_ref=src, dst_ref=dst, send_sem=self.send_sems.at[slot], recv_sem=self.recv_sems.at[slot],
            device_id=device, device_id_type=MESH)

    def send(self, slot, src, dst, device):
        made = self.copy(slot, src, dst, device)
        made.start()
        self.sent.append(made)

    def arrived(self, slot, dst, device):
        self.copy(slot, dst, dst, device).wait_recv()

    def drain(self):
        for made in self.sent:
            made.wait_send()
        self.sent = []


class Ring:
    def __init__(self, links, axis, size, pos, device):
        self.links, self.axis, self.size, self.pos, self.device = links, axis, size, pos, device

    def at(self, delta):
        return lax.rem(self.pos + (delta % self.size), self.size)


class ReduceScatter:
    def __init__(self, ring, own, landing, kib):
        self.ring, self.own, self.landing, self.kib = ring, own, landing, kib
        self.half_ring = ring.size // 2
        self.slots = {(d, kind, t): ring.links.slot()
                      for t in range(1, self.half_ring + 1) for d in (0, 1) for kind in (0, 1)
                      if not (kind == 1 and t == self.half_ring)}

    def wait(self, d, kind, t):
        sign = (-1, 1)[d]
        buf = self.landing.at[d, kind, t - 1]
        self.ring.links.arrived(self.slots[d, kind, t], buf, self.ring.device(sign))
        return buf

    def step(self, t, kind):
        for d, sign in ((0, -1), (1, 1)):
            dist = self.half_ring + 1 - t - kind
            mine = self.own(self.ring.at(sign * dist), d if kind == 0 else 1 - d)
            if t == 1:
                src = mine
            else:
                src = self.wait(d, kind, t - 1)
                src[...] = src[...] + mine[...]
            self.ring.links.send(self.slots[d, kind, t], src, self.landing.at[d, kind, t - 1],
                                 self.ring.device(sign))
        return self.ring.links.clock.sent(self.ring.axis, self.kib)

    def flow(self):
        due = {}
        for t in range(1, self.half_ring + 1):
            for kind in (0, 1):
                if (0, kind, t) not in self.slots:
                    continue
                if t > 1:
                    yield due[kind]
                due[kind] = self.step(t, kind)
        yield max(due.values())
        last = self.half_ring
        out = []
        for h in (0, 1):
            far = self.wait(h, 0, last)
            near = self.wait(1 - h, 1, last - 1)
            out.append(self.own(self.ring.pos, h)[...] + far[...] + near[...])
        return out


class AllGather:
    def __init__(self, ring, full, half, kib):
        self.ring, self.full, self.half, self.kib = ring, full, half, kib
        self.half_ring = ring.size // 2
        self.slots = {(d, t): ring.links.slot() for t in range(1, self.half_ring + 1) for d in (0, 1)}

    def view(self, d, t, owner):
        return self.half(owner, d) if t == self.half_ring else self.full(owner)

    def wait(self, d, t):
        sign = (-1, 1)[d]
        dst = self.view(d, t, self.ring.at(-sign * t))
        self.ring.links.arrived(self.slots[d, t], dst, self.ring.device(sign))

    def step(self, t):
        for d, sign in ((0, -1), (1, 1)):
            if t > 1:
                self.wait(d, t - 1)
            src = self.view(d, t, self.ring.at(-sign * (t - 1)))
            self.ring.links.send(self.slots[d, t], src, src, self.ring.device(sign))
        return self.ring.links.clock.sent(self.ring.axis, self.kib if t < self.half_ring else self.kib / 2)

    def final(self):
        for d in (0, 1):
            self.wait(d, self.half_ring)

    def flow(self, reached=None):
        for t in range(1, self.half_ring + 1):
            due = self.step(t)
            if reached is not None:
                reached(t - 1)
            yield due
        self.final()
        if reached is not None:
            reached(self.half_ring)


class Direct:
    def __init__(self, ring, source, target):
        self.ring, self.target = ring, target
        order = sorted(range(1, ring.size), key=lambda d: -min(d, ring.size - d))
        self.slots = {d: ring.links.slot() for d in order}
        for d in order:
            ring.links.send(self.slots[d], source(ring.at(d)), target(ring.pos), ring.device(d))

    def final(self):
        for d, slot in self.slots.items():
            self.ring.links.arrived(slot, self.target(self.ring.at(-d)), self.ring.device(d))


def place():
    y, s, c = lax.axis_index("view"), lax.axis_index("sent"), lax.axis_index("col")
    return y, s // NZ, lax.rem(s, NZ), c


def rings(links, x, z, y):
    def x_dev(delta):
        return {"sent": lax.rem(x + (delta % NX), NX) * NZ + z}

    def z_dev(delta):
        return {"sent": x * NZ + lax.rem(z + (delta % NZ), NZ)}

    def y_dev(delta):
        return {"view": lax.rem(y + (delta % NY), NY)}

    return (Ring(links, "x", NX, x, x_dev), Ring(links, "z", NZ, z, z_dev), Ring(links, "y", NY, y, y_dev))


def nt(a, b):
    return lax.dot_general(a, b, (((1,), (1,)), ((), ())), precision=HIGH, preferred_element_type=F32)


def nn(a, b):
    return lax.dot_general(a, b, (((1,), (0,)), ((), ())), precision=HIGH, preferred_element_type=F32)


def project(scale, widths, shared, inv, sketched, loadings, merged, gram,
            feats, sharedT, terms, land_x, quarter, land_z, land_z2, quarter2, land_x2, proj, invx,
            part, part_in, part_sum, land_h, half, back, land_b, loadT, stage,
            contrib, mine_in, mine_sum, land_m, outer, outer_in, outer_sum, from_y, over_x, over_z,
            send_sems, recv_sems, feat_sems, out_sems, own_sem):
    y, x, z, c = place()
    links = Links(send_sems, recv_sems)
    clock = links.clock
    rx, rz, ry = rings(links, x, z, y)
    partner = {"col": 1 - c}

    barrier = pltpu.get_barrier_semaphore()
    peers = [partner] + [ring.device(d) for ring in (rx, rz, ry) for d in range(1, ring.size)]
    for peer in peers:
        pl.semaphore_signal(barrier, inc=1, device_id=peer, device_id_type=MESH)

    quarters = [rx.at(d) for d in (2, 3, 1, 0)]
    loads = {}
    for i, v in enumerate((2, 0, 1)):
        for n, q in enumerate(quarters):
            loads[v, n] = pltpu.make_async_copy(
                sketched.at[v, :, pl.ds(pl.multiple_of(q * 256, 256), 256)], feats.at[v, q],
                feat_sems.at[4 * i + n])
            loads[v, n].start()
    own_inv = pltpu.make_async_copy(
        inv.at[:, :, pl.ds(pl.multiple_of(x * 256, 256), 256)], invx.at[:, x], own_sem)
    own_inv.start()
    sharedT[...] = shared[...].T

    first_col = c * 1024 + x * 256
    lane = lax.broadcasted_iota(jnp.int32, (16, 256), 1)
    row = (lane // 64) * (64 * NZ) + z * 64 + lax.rem(lane, 64)

    def lanes_kept(v, value):
        return jnp.where(first_col + lane < widths[v], value, 0.0)

    inv_slots = {}

    def send_inv():
        for d in (1, 3, 2):
            inv_slots[d] = links.slot()
            links.send(inv_slots[d], inv.at[:, :, pl.ds(pl.multiple_of(rx.at(d) * 256, 256), 256)],
                       invx.at[:, x], rx.device(d))
        clock.sent("x", 288)
        yield clock.now

    def need_inv():
        if None not in inv_slots:
            own_inv.wait()
            for d in (1, 3, 2):
                links.arrived(inv_slots[d], invx.at[:, rx.at(-d)], rx.device(d))
            inv_slots[None] = None

    def swap(src, dst, landed):
        slot = links.slot()
        links.send(slot, src, dst, partner)
        yield clock.sent("c", 128)
        links.arrived(slot, landed, partner)

    outs = []

    def use(v, q):
        block = loadT[v, q].reshape(256, 256).T
        stage[v, q] = block
        out = pltpu.make_async_copy(
            stage.at[v, q], loadings.at[v, pl.ds(pl.multiple_of(q * 256, 256), 256)], out_sems.at[len(outs)])
        out.start()
        product = jnp.dot(feats[v, q], block.astype(BF16), preferred_element_type=F32).reshape(2, NY, 128, 256)
        contrib[...] = contrib[...] + product if outs else product
        outs.append(out)

    def reached_x(v, t):
        for d in sorted({t % NX, -t % NX}):
            use(v, rx.at(d))

    def view_flow(v):
        for n, q in enumerate(quarters):
            loads[v, n].wait()
            terms[v, q] = jnp.dot(sharedT[...], feats[v, q], preferred_element_type=F32).reshape(NZ, 32, 256)
        if v == 2:
            pl.semaphore_wait(barrier, len(peers))
            halves = yield from ReduceScatter(
                rz, lambda o, h: terms.at[2, :, o, pl.ds(16 * h, 16)], land_z2, 64).flow()
            for h in (0, 1):
                quarter2[:, pl.ds(16 * h, 16)] = halves[h]
            halves = yield from ReduceScatter(rx, lambda o, h: quarter2.at[o, pl.ds(16 * h, 16)], land_x2, 16).flow()
        else:
            halves = yield from ReduceScatter(
                rx, lambda o, h: terms.at[v, o, pl.ds(4 * h, 4)], land_x.at[v], 128).flow()
            for h in (0, 1):
                quarter[v, pl.ds(4 * h, 4)] = halves[h]
            halves = yield from ReduceScatter(
                rz, lambda o, h: quarter.at[v, o, pl.ds(16 * h, 16)], land_z.at[v], 16).flow()
        for h in (0, 1):
            proj[v, z, pl.ds(16 * h, 16)] = lanes_kept(v, halves[h] * scale)
        yield from AllGather(rz, lambda o: proj.at[v, o], lambda o, h: proj.at[v, o, pl.ds(16 * h, 16)], 32).flow()

        need_inv()
        part[v] = nt(proj[v].reshape(256, 256), invx[v].reshape(256, 256)).reshape(2, NX, 32, 256)
        yield from swap(part.at[v, 1 - c], part_in.at[v], part_in.at[v])
        part_sum[v] = part[v, c] + part_in[v]
        halves = yield from ReduceScatter(
            rx, lambda o, h: part_sum.at[v, o, pl.ds(16 * h, 16)], land_h.at[v], 16).flow()
        for h in (0, 1):
            half[v, c, x, pl.ds(16 * h, 16)] = jnp.where(row < widths[v], halves[h], 0.0)
        yield from AllGather(rx, lambda o: half.at[v, c, o], lambda o, h: half.at[v, c, o, pl.ds(16 * h, 16)], 32).flow()
        yield from swap(half.at[v, c], half.at[v, c], half.at[v, 1 - c])

        back[v] = nn(half[v].reshape(256, 256), invx[v].reshape(256, 256)).reshape(NZ, 32, 256)
        halves = yield from ReduceScatter(
            rz, lambda o, h: back.at[v, o, pl.ds(16 * h, 16)], land_b.at[v], 16).flow()
        for h in (0, 1):
            loadT[v, x, z, pl.ds(16 * h, 16)] = lanes_kept(v, halves[h])
        if v == 2:
            yield from AllGather(rx, lambda o: loadT.at[2, o, z], lambda o, h: loadT.at[2, o, z, pl.ds(16 * h, 16)], 32).flow()
            yield from AllGather(rz, lambda o: loadT.at[2, :, o], lambda o, h: loadT.at[2, :, o, pl.ds(16 * h, 16)], 128).flow()
            for q in range(NX):
                use(2, q)
        else:
            yield from AllGather(rz, lambda o: loadT.at[v, x, o], lambda o, h: loadT.at[v, x, o, pl.ds(16 * h, 16)], 32).flow()
            yield from AllGather(
                rx, lambda o: loadT.at[v, o], lambda o, h: loadT.at[v, o, pl.ds(4 * h, 4)], 256,
            ).flow(lambda t: reached_x(v, t))

    clock.add(0.0, view_flow(2))
    clock.add(0.5, view_flow(0))
    clock.add(5.5, view_flow(1))
    clock.add(16.0, send_inv())
    clock.run()

    def now(flow):
        try:
            while True:
                next(flow)
        except StopIteration as stop:
            return stop.value

    now(swap(contrib.at[1 - c], mine_in, mine_in))
    mine_sum[...] = contrib[c] + mine_in[...]
    halves = now(ReduceScatter(ry, lambda o, h: mine_sum.at[o, pl.ds(64 * h, 64)], land_m, 64).flow())
    for h in (0, 1):
        merged[c, y, pl.ds(64 * h, 64)] = halves[h]
    rows = merged[c, y]
    outer[...] = tn(rows, rows).reshape(2, NY, 32, 256)
    now(swap(outer.at[1 - c], outer_in, outer_in))
    outer_sum[...] = outer[c] + outer_in[...]
    gs = Direct(ry, lambda o: outer_sum.at[o], lambda o: from_y.at[o])
    mg = AllGather(ry, lambda o: merged.at[c, o], lambda o, h: merged.at[c, o, pl.ds(64 * h, 64)], 128)
    from_y[y] = outer_sum[y]
    gs.final()
    mg.step(1)
    over_x[x] = (from_y[0] + from_y[1]) + (from_y[2] + from_y[3])
    Direct(rx, lambda o: over_x.at[x], lambda o: over_x.at[o]).final()
    over_z[z] = (over_x[0] + over_x[1]) + (over_x[2] + over_x[3])
    gz = Direct(rz, lambda o: over_z.at[z], lambda o: over_z.at[o])
    mg.step(2)
    mg.final()
    slot = links.slot()
    links.send(slot, merged.at[c], merged.at[c], partner)
    gz.final()
    acc = over_z[0]
    for i in range(1, NZ):
        acc = acc + over_z[i]
    gram[c, y] = acc
    Direct(ry, lambda o: gram.at[c, y], lambda o: gram.at[c, o]).final()
    now(swap(gram.at[c], gram.at[c], gram.at[1 - c]))
    links.arrived(slot, merged.at[1 - c], partner)
    links.drain()
    for out in outs:
        out.wait()


PANEL = 32


def panel_inverse(tiles, lane0):
    groups = PANEL // 8
    sub = lax.broadcasted_iota(jnp.int32, (8, 128), 0)
    lane = lax.broadcasted_iota(jnp.int32, (8, 128), 1)

    def spread(tile, s):
        return jnp.broadcast_to(tile[s:s + 1, :], (8, 128))

    cols = [{g: jnp.broadcast_to(tiles[g][:, lane0 + j:lane0 + j + 1], (8, 128)) for g in range(j // 8, groups)}
            for j in range(PANEL)]
    unit = [jnp.where(lane == sub + 8 * g, 1.0, 0.0).astype(F32) for g in range(groups)]
    pivots = [jnp.ones((8, 128), F32) for g in range(groups)]
    for k in range(PANEL):
        gk, sk = divmod(k, 8)
        pivot = spread(cols[k][gk], sk)
        inverse = 1.0 / pivot
        pivots[gk] = jnp.where(sub == sk, pivot, pivots[gk])
        mult = {g: cols[k][g] * inverse for g in range(gk, groups)}
        for j in range(k + 1, PANEL):
            gj, sj = divmod(j, 8)
            entry = spread(cols[k][gj], sj)
            for g in range(gj, groups):
                cols[j][g] = cols[j][g] - mult[g] * entry
        row = spread(unit[gk], sk)
        for g in range(gk, groups):
            m = jnp.where(sub > sk, mult[g], 0.0) if g == gk else mult[g]
            unit[g] = unit[g] - m * row
    return jnp.concatenate([unit[g] * lax.rsqrt(pivots[g]) for g in range(groups)], axis=0)[:, :PANEL]


def tn(a, b):
    return lax.dot_general(a, b, (((0,), (0,)), ((), ())), precision=HIGH, preferred_element_type=F32)


def factor_inverse(work, inverse, between):
    n = work.shape[0]
    for p in range(n // PANEL):
        r0 = p * PANEL
        lt = r0 // 128 * 128
        tiles = [work[r0 + 8 * g:r0 + 8 * g + 8, lt:lt + 128] for g in range(PANEL // 8)]
        block = panel_inverse(tiles, r0 - lt)
        col = lax.broadcasted_iota(jnp.int32, (PANEL, n), 1)
        row = lax.broadcasted_iota(jnp.int32, (PANEL, n), 0)
        here = (col >= r0) & (col < r0 + PANEL)
        wide = jnp.where(here, jnp.where(col == row + r0, 1.0, 0.0), work[r0:r0 + PANEL, :])
        u = nn(block, wide)
        inverse[r0:r0 + PANEL, :] = jnp.where(col < r0 + PANEL, u, 0.0)
        between(p)
        r1 = r0 + PANEL
        if r1 < n:
            base = r1 // 128 * 128
            upd = tn(u[:, base:], u)[r1 - base:]
            col = lax.broadcasted_iota(jnp.int32, (n - r1, n), 1)
            here = (col >= r0) & (col < r1)
            work[r1:, :] = jnp.where(here, 0.0, work[r1:, :]) - upd


def solve(root, gram, merged, loaded, updated, loadings, work, inverse, passing, in_sem, out_sem):
    bring = pltpu.make_async_copy(loaded, passing, in_sem)
    put = pltpu.make_async_copy(passing, loadings, out_sem)
    bring.start()
    work[...] = gram[...]

    def between(panel):
        if panel == 2:
            bring.wait()
            put.start()

    factor_inverse(work, inverse, between)
    updated[...] = nt(merged[...], inverse[...]) * root
    put.wait()


def shards(sketched, widths, inv_factor, shared):
    total_rows = shared.shape[0] * lax.axis_size("sent")
    vmem, smem, anywhere = (pl.BlockSpec(memory_space=m) for m in (pltpu.VMEM, pltpu.SMEM, pl.ANY))

    def buf(*shape):
        return pltpu.VMEM(shape, F32)

    sems = [pltpu.SemaphoreType.DMA((SEMS,)), pltpu.SemaphoreType.DMA((SEMS,))]

    def kernel_a(*refs):
        project(1.0 / math.sqrt(total_rows), *refs)

    loadings, merged, gram = pl.pallas_call(
        kernel_a,
        name="project",
        out_shape=(jax.ShapeDtypeStruct((3, 1024, 256), F32), jax.ShapeDtypeStruct((2, NY, 128, 256), F32),
                   jax.ShapeDtypeStruct((2, NY, 32, 256), F32)),
        in_specs=[smem, vmem, vmem, anywhere],
        out_specs=(anywhere, vmem, vmem),
        scratch_shapes=[
            pltpu.VMEM((3, 4, 1024, 256), BF16), pltpu.VMEM((256, 1024), BF16),
            buf(3, 4, 8, 32, 256), buf(2, 2, 2, 2, 4, 32, 256), buf(2, 8, 32, 256), buf(2, 2, 2, 4, 16, 256),
            buf(2, 2, 4, 4, 16, 256), buf(4, 32, 256), buf(2, 2, 2, 16, 256), buf(3, 8, 32, 256),
            buf(3, 4, 64, 256), buf(3, 2, 4, 32, 256), buf(3, 4, 32, 256), buf(3, 4, 32, 256),
            buf(3, 2, 2, 2, 16, 256), buf(3, 2, 4, 32, 256), buf(3, 8, 32, 256), buf(3, 2, 2, 4, 16, 256),
            buf(3, 4, 8, 32, 256), buf(3, 4, 256, 256),
            buf(2, 4, 128, 256), buf(4, 128, 256), buf(4, 128, 256), buf(2, 2, 2, 64, 256), buf(2, 4, 32, 256),
            buf(4, 32, 256), buf(4, 32, 256), buf(4, 32, 256), buf(4, 32, 256), buf(8, 32, 256), *sems,
            pltpu.SemaphoreType.DMA((12,)), pltpu.SemaphoreType.DMA((12,)), pltpu.SemaphoreType.DMA],
        compiler_params=pltpu.CompilerParams(collective_id=0, has_side_effects=True, vmem_limit_bytes=56 * 2**20),
    )(widths, shared, inv_factor, sketched)
    merged, gram = merged.reshape(1024, 256), gram.reshape(256, 256)

    def kernel_c(*refs):
        solve(math.sqrt(total_rows), *refs)

    updated, loadings = pl.pallas_call(
        kernel_c,
        name="solve",
        out_shape=(jax.ShapeDtypeStruct((1024, 256), F32), jax.ShapeDtypeStruct((3, 1024, 256), F32)),
        in_specs=[vmem, vmem, anywhere],
        out_specs=(vmem, anywhere),
        scratch_shapes=[buf(256, 256), buf(256, 256), buf(3, 1024, 256),
                        pltpu.SemaphoreType.DMA, pltpu.SemaphoreType.DMA],
        compiler_params=pltpu.CompilerParams(vmem_limit_bytes=32 * 2**20),
    )(gram, merged, loadings)
    return (loadings, updated)


def solution(mesh):
    return jax.shard_map(
        shards,
        mesh=mesh,
        in_specs=(P("view", "sent", "col"), P("view"), P("view", "sent", "col"), P("sent", None)),
        out_specs=(P("view", "col", None), P("sent", None)),
        check_vma=False,
    )
```

```python
import math

import jax
import jax.numpy as jnp
from jax import lax
from jax.experimental import pallas as pl
from jax.experimental.pallas import tpu as pltpu
from jax.sharding import PartitionSpec as P

MESH = pl.DeviceIdType.MESH
HIGH = lax.Precision.HIGHEST
F32 = jnp.float32
BF16 = jnp.bfloat16
NX, NZ, NY = 4, 8, 4
SEMS = 448


class Clock:
    def __init__(self):
        self.now, self.busy, self.flows = 0.0, {}, []

    def sent(self, axis, kib):
        rate = 0.0087 if axis == "c" else 0.0225
        self.busy[axis] = max(self.now, self.busy.get(axis, 0.0)) + kib * rate
        return self.busy[axis] + (1.0 if axis == "c" else 1.9)

    def add(self, start, flow):
        self.flows.append([start, len(self.flows), flow])

    def run(self):
        while self.flows:
            item = min(self.flows)
            self.now = max(self.now, item[0]) + 0.08
            try:
                item[0] = next(item[2])
            except StopIteration:
                self.flows.remove(item)


class Links:
    def __init__(self, send_sems, recv_sems):
        self.send_sems, self.recv_sems, self.used, self.sent = send_sems, recv_sems, 0, []
        self.clock = Clock()

    def slot(self):
        self.used += 1
        assert self.used <= SEMS
        return self.used - 1

    def copy(self, slot, src, dst, device):
        return pltpu.make_async_remote_copy(
            src_ref=src, dst_ref=dst, send_sem=self.send_sems.at[slot], recv_sem=self.recv_sems.at[slot],
            device_id=device, device_id_type=MESH)

    def send(self, slot, src, dst, device):
        made = self.copy(slot, src, dst, device)
        made.start()
        self.sent.append(made)

    def arrived(self, slot, dst, device):
        self.copy(slot, dst, dst, device).wait_recv()

    def drain(self):
        for made in self.sent:
            made.wait_send()
        self.sent = []


class Ring:
    def __init__(self, links, axis, size, pos, device):
        self.links, self.axis, self.size, self.pos, self.device = links, axis, size, pos, device

    def at(self, delta):
        return lax.rem(self.pos + (delta % self.size), self.size)


class ReduceScatter:
    def __init__(self, ring, own, landing, kib):
        self.ring, self.own, self.landing, self.kib = ring, own, landing, kib
        self.half_ring = ring.size // 2
        self.slots = {(d, kind, t): ring.links.slot()
                      for t in range(1, self.half_ring + 1) for d in (0, 1) for kind in (0, 1)
                      if not (kind == 1 and t == self.half_ring)}

    def wait(self, d, kind, t):
        sign = (-1, 1)[d]
        buf = self.landing.at[d, kind, t - 1]
        self.ring.links.arrived(self.slots[d, kind, t], buf, self.ring.device(sign))
        return buf

    def step(self, t, kind):
        for d, sign in ((0, -1), (1, 1)):
            dist = self.half_ring + 1 - t - kind
            mine = self.own(self.ring.at(sign * dist), d if kind == 0 else 1 - d)
            if t == 1:
                src = mine
            else:
                src = self.wait(d, kind, t - 1)
                src[...] = src[...] + mine[...]
            self.ring.links.send(self.slots[d, kind, t], src, self.landing.at[d, kind, t - 1],
                                 self.ring.device(sign))
        return self.ring.links.clock.sent(self.ring.axis, self.kib)

    def flow(self):
        due = {}
        for t in range(1, self.half_ring + 1):
            for kind in (0, 1):
                if (0, kind, t) not in self.slots:
                    continue
                if t > 1:
                    yield due[kind]
                due[kind] = self.step(t, kind)
        yield max(due.values())
        return self.final()

    def final(self):
        last = self.half_ring
        out = []
        for h in (0, 1):
            far = self.wait(h, 0, last)
            near = self.wait(1 - h, 1, last - 1)
            out.append(self.own(self.ring.pos, h)[...] + far[...] + near[...])
        return out


class AllGather:
    def __init__(self, ring, full, half, kib):
        self.ring, self.full, self.half, self.kib = ring, full, half, kib
        self.half_ring = ring.size // 2
        self.slots = {(d, t): ring.links.slot() for t in range(1, self.half_ring + 1) for d in (0, 1)}

    def view(self, d, t, owner):
        return self.half(owner, d) if t == self.half_ring else self.full(owner)

    def wait(self, d, t):
        sign = (-1, 1)[d]
        dst = self.view(d, t, self.ring.at(-sign * t))
        self.ring.links.arrived(self.slots[d, t], dst, self.ring.device(sign))

    def step(self, t):
        for d, sign in ((0, -1), (1, 1)):
            if t > 1:
                self.wait(d, t - 1)
            src = self.view(d, t, self.ring.at(-sign * (t - 1)))
            self.ring.links.send(self.slots[d, t], src, src, self.ring.device(sign))
        return self.ring.links.clock.sent(self.ring.axis, self.kib if t < self.half_ring else self.kib / 2)

    def final(self):
        for d in (0, 1):
            self.wait(d, self.half_ring)

    def flow(self, reached=None):
        for t in range(1, self.half_ring + 1):
            due = self.step(t)
            if reached is not None:
                reached(t - 1)
            yield due
        self.final()
        if reached is not None:
            reached(self.half_ring)


class Direct:
    def __init__(self, ring, source, target):
        self.ring, self.target = ring, target
        order = sorted(range(1, ring.size), key=lambda d: -min(d, ring.size - d))
        self.slots = {d: ring.links.slot() for d in order}
        for d in order:
            ring.links.send(self.slots[d], source(ring.at(d)), target(ring.pos), ring.device(d))

    def final(self):
        for d, slot in self.slots.items():
            self.ring.links.arrived(slot, self.target(self.ring.at(-d)), self.ring.device(d))


def place():
    y, s, c = lax.axis_index("view"), lax.axis_index("sent"), lax.axis_index("col")
    return y, s // NZ, lax.rem(s, NZ), c


def rings(links, x, z, y):
    def x_dev(delta):
        return {"sent": lax.rem(x + (delta % NX), NX) * NZ + z}

    def z_dev(delta):
        return {"sent": x * NZ + lax.rem(z + (delta % NZ), NZ)}

    def y_dev(delta):
        return {"view": lax.rem(y + (delta % NY), NY)}

    return (Ring(links, "x", NX, x, x_dev), Ring(links, "z", NZ, z, z_dev), Ring(links, "y", NY, y, y_dev))


def nt(a, b):
    return lax.dot_general(a, b, (((1,), (1,)), ((), ())), precision=HIGH, preferred_element_type=F32)


def nn(a, b):
    return lax.dot_general(a, b, (((1,), (0,)), ((), ())), precision=HIGH, preferred_element_type=F32)


CHAINS = (
    (0, 0, 0.0, "x", "z"), (0, 1, 0.01, "z", "z"), (1, 0, 0.02, "x", "z"),
    (1, 1, 1.0, "z", "x"), (2, 0, 3.0, "x", "x"), (2, 1, 9.0, "z", "x"),
)
INV_START = 12.0


def project(scale, widths, shared, inv, sketched, stage, merged, gram,
            feats, sharedH, sharedT, terms, land_x, land_xz, land_z, land_zx, quarter, slab, proj, invx, hop,
            part, part_in, part_sum, land_h, half, back, land_b, loadT,
            contrib, mine_in, mine_sum, land_m, outer, outer_in, outer_sum, from_y, over_x, over_z,
            send_sems, recv_sems, feat_sems, own_sems):
    y, x, z, c = place()
    links = Links(send_sems, recv_sems)
    clock = links.clock
    rx, rz, ry = rings(links, x, z, y)
    partner = {"col": 1 - c}

    bring_shared = pltpu.make_async_copy(shared, sharedH, own_sems.at[0])
    bring_shared.start()
    barrier = pltpu.get_barrier_semaphore()
    peers = [partner] + [ring.device(d) for ring in (rx, rz, ry) for d in range(1, ring.size)]
    for peer in peers:
        pl.semaphore_signal(barrier, inc=1, device_id=peer, device_id_type=MESH)

    def columns(q):
        return pl.ds(pl.multiple_of(q * 256, 256), 256)

    quarters = [rx.at(d) for d in (2, 3, 1, 0)]
    loads = {}
    for v in range(3):
        for n, q in enumerate(quarters):
            loads[v, n] = pltpu.make_async_copy(sketched.at[v, :, columns(q)], feats.at[v, q], feat_sems.at[4 * v + n])
            loads[v, n].start()
    own_inv = pltpu.make_async_copy(inv.at[:, :, columns(x)], invx.at[:, x], own_sems.at[1])
    own_inv.start()
    bring_shared.wait()
    sharedT[...] = sharedH[...].T

    first_col = c * 1024 + x * 256
    lane = lax.broadcasted_iota(jnp.int32, (8, 256), 1)
    row = (lane // 64) * (64 * NZ) + z * 64 + lax.rem(lane, 64)

    def lanes_kept(v, value):
        return jnp.where(first_col + lane < widths[v], value, 0.0)

    inv_slots = {(v, kind, i): links.slot() for v in range(3) for kind in ("near", "hop", "far") for i in (0, 1)}

    def inv_flow():
        for v in range(3):
            for i, sign in enumerate((1, -1)):
                links.send(inv_slots[v, "near", i], inv.at[v, :, columns(rx.at(sign))], invx.at[v, x], rx.device(sign))
                links.send(inv_slots[v, "hop", i], inv.at[v, pl.ds(32 * i, 32), columns(rx.at(2))],
                           hop.at[v, i], rx.device(sign))
            due = clock.sent("x", 96)
            yield clock.now
        yield due
        for v in range(3):
            for i, sign in enumerate((1, -1)):
                links.arrived(inv_slots[v, "hop", i], hop.at[v, i], rx.device(sign))
                links.send(inv_slots[v, "far", i], hop.at[v, i], invx.at[v, rx.at(-sign), pl.ds(32 * i, 32)],
                           rx.device(sign))
            due = clock.sent("x", 32)
            yield clock.now

    sending_inv = inv_flow()
    inv_here = set()

    def need_inv(v):
        for _ in sending_inv:
            pass
        if not inv_here:
            own_inv.wait()
        if v not in inv_here:
            inv_here.add(v)
            for i, sign in enumerate((1, -1)):
                links.arrived(inv_slots[v, "near", i], invx.at[v, rx.at(-sign)], rx.device(sign))
                links.arrived(inv_slots[v, "far", i], invx.at[v, rx.at(2), pl.ds(32 * i, 32)], rx.device(sign))

    def swap(src, dst, landed):
        slot = links.slot()
        links.send(slot, src, dst, partner)
        yield clock.sent("c", 64)
        links.arrived(slot, landed, partner)

    used = []

    def use(v, k, q):
        block = loadT[v, k, q].reshape(128, 256).T
        stage[v, columns(q), 128 * k:128 * k + 128] = block
        product = jnp.dot(feats[v, q], block.astype(BF16), preferred_element_type=F32).reshape(2, NY, 128, 128)
        here = slice(128 * k, 128 * k + 128)
        contrib[:, :, :, here] = contrib[:, :, :, here] + product if k in used else product
        used.append(k)

    made = set()

    def make_terms(v):
        if v in made:
            return
        made.add(v)
        for n, q in enumerate(quarters):
            loads[v, n].wait()
            terms[v, :, q] = jnp.dot(sharedT[...], feats[v, q], preferred_element_type=F32).reshape(2, NZ, 16, 256)
        if len(made) == 1:
            pl.semaphore_wait(barrier, len(peers))

    def chain(v, k, first, last):
        make_terms(v)
        if first == "x":
            halves = yield from ReduceScatter(
                rx, lambda o, h: terms.at[v, k, o, pl.ds(4 * h, 4)], land_x.at[v, k], 64).flow()
            for h in (0, 1):
                quarter[v, k, pl.ds(4 * h, 4)] = halves[h]
            halves = yield from ReduceScatter(
                rz, lambda o, h: quarter.at[v, k, o, pl.ds(8 * h, 8)], land_xz.at[v, k], 8).flow()
        else:
            halves = yield from ReduceScatter(
                rz, lambda o, h: terms.at[v, k, :, o, pl.ds(8 * h, 8)], land_z.at[v, k], 32).flow()
            for h in (0, 1):
                slab[v, k, :, pl.ds(8 * h, 8)] = halves[h]
            halves = yield from ReduceScatter(
                rx, lambda o, h: slab.at[v, k, o, pl.ds(8 * h, 8)], land_zx.at[v, k], 8).flow()
        for h in (0, 1):
            proj[v, k, z, pl.ds(8 * h, 8)] = lanes_kept(v, halves[h] * scale)
        yield from AllGather(
            rz, lambda o: proj.at[v, k, o], lambda o, h: proj.at[v, k, o, pl.ds(8 * h, 8)], 16).flow()

        need_inv(v)
        part[v, k] = nt(proj[v, k].reshape(128, 256), invx[v].reshape(256, 256)).reshape(2, NX, 16, 256)
        yield from swap(part.at[v, k, 1 - c], part_in.at[v, k], part_in.at[v, k])
        part_sum[v, k] = part[v, k, c] + part_in[v, k]
        halves = yield from ReduceScatter(
            rx, lambda o, h: part_sum.at[v, k, o, pl.ds(8 * h, 8)], land_h.at[v, k], 8).flow()
        for h in (0, 1):
            half[v, k, c, x, pl.ds(8 * h, 8)] = jnp.where(row < widths[v], halves[h], 0.0)
        yield from AllGather(
            rx, lambda o: half.at[v, k, c, o], lambda o, h: half.at[v, k, c, o, pl.ds(8 * h, 8)], 16).flow()
        yield from swap(half.at[v, k, c], half.at[v, k, c], half.at[v, k, 1 - c])

        back[v, k] = nn(half[v, k].reshape(128, 256), invx[v].reshape(256, 256)).reshape(NZ, 16, 256)
        halves = yield from ReduceScatter(
            rz, lambda o, h: back.at[v, k, o, pl.ds(8 * h, 8)], land_b.at[v, k], 8).flow()
        for h in (0, 1):
            loadT[v, k, x, z, pl.ds(8 * h, 8)] = lanes_kept(v, halves[h])
        if last == "x":
            yield from AllGather(
                rx, lambda o: loadT.at[v, k, o, z], lambda o, h: loadT.at[v, k, o, z, pl.ds(8 * h, 8)], 16).flow()
            yield from AllGather(
                rz, lambda o: loadT.at[v, k, :, o], lambda o, h: loadT.at[v, k, :, o, pl.ds(8 * h, 8)], 64).flow()
            for q in range(NX):
                use(v, k, q)
        else:
            yield from AllGather(
                rz, lambda o: loadT.at[v, k, x, o], lambda o, h: loadT.at[v, k, x, o, pl.ds(8 * h, 8)], 16).flow()

            def reached(t):
                for d in sorted({t % NX, -t % NX}):
                    use(v, k, rx.at(d))

            yield from AllGather(
                rx, lambda o: loadT.at[v, k, o], lambda o, h: loadT.at[v, k, o, pl.ds(4 * h, 4)], 128).flow(reached)

    for v, k, start, first, last in CHAINS:
        clock.add(start, chain(v, k, first, last))
    clock.add(INV_START, sending_inv)
    clock.run()

    slots = {d: links.slot() for d in (2, 1, 3, 0)}
    for d, slot in slots.items():
        links.send(slot, contrib.at[1 - c, ry.at(d)], mine_in.at[ry.at(d)], partner)

    def summed(d):
        o = ry.at(d)
        links.arrived(slots[d], mine_in.at[o], partner)
        mine_sum[o] = contrib[c, o] + mine_in[o]

    ms = ReduceScatter(ry, lambda o, h: mine_sum.at[o, pl.ds(64 * h, 64)], land_m, 64)
    summed(2)
    ms.step(1, 0)
    summed(1)
    summed(3)
    ms.step(1, 1)
    summed(0)
    ms.step(2, 0)
    halves = ms.final()
    for h in (0, 1):
        merged[c, y, pl.ds(64 * h, 64)] = halves[h]
    rows = merged[c, y]

    outer[...] = tn(rows, rows).reshape(2, NY, 32, 256)
    slot = links.slot()
    links.send(slot, outer.at[1 - c], outer_in, partner)
    links.arrived(slot, outer_in, partner)
    outer_sum[...] = outer[c] + outer_in[...]
    gs = Direct(ry, lambda o: outer_sum.at[o], lambda o: from_y.at[o])
    mg = AllGather(ry, lambda o: merged.at[c, o], lambda o, h: merged.at[c, o, pl.ds(64 * h, 64)], 128)
    from_y[y] = outer_sum[y]
    gs.final()
    mg.step(1)
    over_x[x] = (from_y[0] + from_y[1]) + (from_y[2] + from_y[3])
    Direct(rx, lambda o: over_x.at[x], lambda o: over_x.at[o]).final()
    over_z[z] = (over_x[0] + over_x[1]) + (over_x[2] + over_x[3])
    gz = Direct(rz, lambda o: over_z.at[z], lambda o: over_z.at[o])
    mg.step(2)
    mg.final()
    slot = links.slot()
    links.send(slot, merged.at[c], merged.at[c], partner)
    gz.final()
    acc = over_z[0]
    for i in range(1, NZ):
        acc = acc + over_z[i]
    gram[c, y] = acc
    Direct(ry, lambda o: gram.at[c, y], lambda o: gram.at[c, o]).final()
    last = links.slot()
    links.send(last, gram.at[c], gram.at[c], partner)
    links.arrived(last, gram.at[1 - c], partner)
    links.arrived(slot, merged.at[1 - c], partner)
    links.drain()


PANEL = 32


def panel_inverse(tiles, lane0):
    groups = PANEL // 8
    sub = lax.broadcasted_iota(jnp.int32, (8, 128), 0)
    lane = lax.broadcasted_iota(jnp.int32, (8, 128), 1)

    def spread(tile, s):
        return jnp.broadcast_to(tile[s:s + 1, :], (8, 128))

    cols = [{g: jnp.broadcast_to(tiles[g][:, lane0 + j:lane0 + j + 1], (8, 128)) for g in range(j // 8, groups)}
            for j in range(PANEL)]
    unit = [jnp.where(lane == sub + 8 * g, 1.0, 0.0).astype(F32) for g in range(groups)]
    pivots = [jnp.ones((8, 128), F32) for g in range(groups)]
    for k in range(PANEL):
        gk, sk = divmod(k, 8)
        pivot = spread(cols[k][gk], sk)
        inverse = 1.0 / pivot
        pivots[gk] = jnp.where(sub == sk, pivot, pivots[gk])
        mult = {g: cols[k][g] * inverse for g in range(gk, groups)}
        for j in range(k + 1, PANEL):
            gj, sj = divmod(j, 8)
            entry = spread(cols[k][gj], sj)
            for g in range(gj, groups):
                cols[j][g] = cols[j][g] - mult[g] * entry
        row = spread(unit[gk], sk)
        for g in range(gk, groups):
            m = jnp.where(sub > sk, mult[g], 0.0) if g == gk else mult[g]
            unit[g] = unit[g] - m * row
    return jnp.concatenate([unit[g] * lax.rsqrt(pivots[g]) for g in range(groups)], axis=0)[:, :PANEL]


def tn(a, b):
    return lax.dot_general(a, b, (((0,), (0,)), ((), ())), precision=HIGH, preferred_element_type=F32)


def factor_inverse(work, inverse):
    n = work.shape[0]
    for p in range(n // PANEL):
        r0 = p * PANEL
        lt = r0 // 128 * 128
        tiles = [work[r0 + 8 * g:r0 + 8 * g + 8, lt:lt + 128] for g in range(PANEL // 8)]
        block = panel_inverse(tiles, r0 - lt)
        col = lax.broadcasted_iota(jnp.int32, (PANEL, n), 1)
        row = lax.broadcasted_iota(jnp.int32, (PANEL, n), 0)
        here = (col >= r0) & (col < r0 + PANEL)
        wide = jnp.where(here, jnp.where(col == row + r0, 1.0, 0.0), work[r0:r0 + PANEL, :])
        u = nn(block, wide)
        inverse[r0:r0 + PANEL, :] = jnp.where(col < r0 + PANEL, u, 0.0)
        r1 = r0 + PANEL
        if r1 < n:
            base = r1 // 128 * 128
            upd = tn(u[:, base:], u)[r1 - base:]
            col = lax.broadcasted_iota(jnp.int32, (n - r1, n), 1)
            here = (col >= r0) & (col < r1)
            work[r1:, :] = jnp.where(here, 0.0, work[r1:, :]) - upd


def solve(root, gram, merged, loaded, updated, loadings, work, inverse, sem):
    put = pltpu.make_async_copy(loaded, loadings, sem)
    put.start()
    work[...] = gram[...]
    factor_inverse(work, inverse)
    updated[...] = nt(merged[...], inverse[...]) * root
    put.wait()


def shards(sketched, widths, inv_factor, shared):
    total_rows = shared.shape[0] * lax.axis_size("sent")
    vmem, smem, hbm = (pl.BlockSpec(memory_space=m) for m in (pltpu.VMEM, pltpu.SMEM, pltpu.HBM))

    def buf(*shape):
        return pltpu.VMEM(shape, F32)

    sems = [pltpu.SemaphoreType.DMA((SEMS,)), pltpu.SemaphoreType.DMA((SEMS,))]

    def kernel_a(*refs):
        project(1.0 / math.sqrt(total_rows), *refs)

    stage, merged, gram = pl.pallas_call(
        kernel_a,
        name="project",
        out_shape=(jax.ShapeDtypeStruct((3, 1024, 256), F32), jax.ShapeDtypeStruct((2, NY, 128, 256), F32),
                   jax.ShapeDtypeStruct((2, NY, 32, 256), F32)),
        in_specs=[smem, hbm, hbm, hbm],
        out_specs=(vmem, vmem, vmem),
        scratch_shapes=[
            pltpu.VMEM((3, 4, 1024, 256), BF16), pltpu.VMEM((1024, 256), BF16), pltpu.VMEM((256, 1024), BF16),
            buf(3, 2, 4, 8, 16, 256), buf(3, 2, 2, 2, 2, 4, 16, 256), buf(3, 2, 2, 2, 4, 8, 256),
            buf(3, 2, 2, 2, 4, 4, 8, 256), buf(3, 2, 2, 2, 2, 8, 256), buf(3, 2, 8, 16, 256), buf(3, 2, 4, 16, 256),
            buf(3, 2, 8, 16, 256), buf(3, 4, 64, 256), buf(3, 2, 32, 256),
            buf(3, 2, 2, 4, 16, 256), buf(3, 2, 4, 16, 256), buf(3, 2, 4, 16, 256), buf(3, 2, 2, 2, 2, 8, 256),
            buf(3, 2, 2, 4, 16, 256), buf(3, 2, 8, 16, 256), buf(3, 2, 2, 2, 4, 8, 256), buf(3, 2, 4, 8, 16, 256),
            buf(2, 4, 128, 256), buf(4, 128, 256), buf(4, 128, 256), buf(2, 2, 2, 64, 256), buf(2, 4, 32, 256),
            buf(4, 32, 256), buf(4, 32, 256), buf(4, 32, 256), buf(4, 32, 256), buf(8, 32, 256), *sems,
            pltpu.SemaphoreType.DMA((12,)), pltpu.SemaphoreType.DMA((2,))],
        compiler_params=pltpu.CompilerParams(collective_id=0, has_side_effects=True, vmem_limit_bytes=44 * 2**20),
    )(widths, shared, inv_factor, sketched)
    merged, gram = merged.reshape(1024, 256), gram.reshape(256, 256)

    def kernel_c(*refs):
        solve(math.sqrt(total_rows), *refs)

    updated, loadings = pl.pallas_call(
        kernel_c,
        name="solve",
        out_shape=(jax.ShapeDtypeStruct((1024, 256), F32), jax.ShapeDtypeStruct((3, 1024, 256), F32)),
        in_specs=[vmem, vmem, vmem],
        out_specs=(vmem, hbm),
        scratch_shapes=[buf(256, 256), buf(256, 256), pltpu.SemaphoreType.DMA],
        compiler_params=pltpu.CompilerParams(vmem_limit_bytes=16 * 2**20),
    )(gram, merged, stage)
    return (loadings, updated)


def solution(mesh):
    return jax.shard_map(
        shards,
        mesh=mesh,
        in_specs=(P("view", "sent", "col"), P("view"), P("view", "sent", "col"), P("sent", None)),
        out_specs=(P("view", "col", None), P("sent", None)),
        check_vma=False,
    )
```

```python
import math

import jax
import jax.numpy as jnp
from jax import lax
from jax.experimental import pallas as pl
from jax.experimental.pallas import tpu as pltpu
from jax.sharding import PartitionSpec as P

MESH = pl.DeviceIdType.MESH
HIGH = lax.Precision.HIGHEST
F32 = jnp.float32
BF16 = jnp.bfloat16
NX, NZ, NY = 4, 8, 4
SEND_SEMS, RECV_SEMS = 40, 224


class Clock:
    def __init__(self):
        self.now, self.busy, self.flows = 0.0, {}, []

    def sent(self, axis, kib, latency=2.4):
        self.busy[axis] = max(self.now, self.busy.get(axis, 0.0)) + kib * 0.0225
        return self.busy[axis] + latency

    def add(self, start, flow):
        self.flows.append([start, len(self.flows), flow])

    def run(self):
        while self.flows:
            item = min(self.flows)
            self.now = max(self.now, item[0]) + 0.1
            try:
                item[0] = next(item[2])
            except StopIteration:
                self.flows.remove(item)


def kib(ref):
    return math.prod(ref.shape) * 4 // 1024


class Links:
    def __init__(self, send_sems, recv_sems, ruler):
        self.send_sems, self.recv_sems, self.ruler = send_sems, recv_sems, ruler
        self.used, self.groups, self.clock = 0, [], Clock()

    def slot(self):
        self.used += 1
        assert self.used <= RECV_SEMS
        return self.used - 1

    def send(self, slot, src, dst, device):
        size = kib(src)
        if not self.groups or self.groups[-1] + size > 1024:
            self.groups.append(0)
            assert len(self.groups) <= SEND_SEMS
        self.groups[-1] += size
        pltpu.make_async_remote_copy(
            src_ref=src, dst_ref=dst, send_sem=self.send_sems.at[len(self.groups) - 1],
            recv_sem=self.recv_sems.at[slot], device_id=device, device_id_type=MESH).start()

    def wait(self, sem, size):
        rows = self.ruler.at[0, pl.ds(0, size)]
        pltpu.make_async_copy(rows, rows, sem).wait()

    def arrived(self, slot, size):
        self.wait(self.recv_sems.at[slot], size)

    def drain(self):
        for group, size in enumerate(self.groups):
            self.wait(self.send_sems.at[group], size)


class Ring:
    def __init__(self, links, axis, size, pos, device):
        self.links, self.axis, self.size, self.pos, self.device = links, axis, size, pos, device

    def at(self, delta):
        return lax.rem(self.pos + (delta % self.size), self.size)


class ReduceScatter:
    def __init__(self, ring, own, landing):
        self.ring, self.own, self.landing = ring, own, landing
        self.kib = kib(landing.at[0, 0, 0])
        self.half_ring = ring.size // 2
        self.slots = {(kind, t): ring.links.slot()
                      for t in range(1, self.half_ring + 1) for kind in (0, 1)
                      if not (kind == 1 and t == self.half_ring)}

    def wait(self, kind, t):
        self.ring.links.arrived(self.slots[kind, t], 2 * self.kib)

    def step(self, t, kind):
        if t > 1:
            self.wait(kind, t - 1)
        for d, sign in ((0, -1), (1, 1)):
            dist = self.half_ring + 1 - t - kind
            src = self.own(self.ring.at(sign * dist), d if kind == 0 else 1 - d)
            if t > 1:
                buf = self.landing.at[d, kind, t - 2]
                buf[...] = buf[...] + src[...]
                src = buf
            self.ring.links.send(self.slots[kind, t], src, self.landing.at[d, kind, t - 1], self.ring.device(sign))
        return self.ring.links.clock.sent(self.ring.axis, self.kib)

    def flow(self):
        due = {}
        for t in range(1, self.half_ring + 1):
            for kind in (0, 1):
                if (kind, t) not in self.slots:
                    continue
                if t > 1:
                    yield due[kind]
                due[kind] = self.step(t, kind)
        yield max(due.values())
        return self.final()

    def final(self):
        last = self.half_ring
        self.wait(0, last)
        self.wait(1, last - 1)
        return [self.own(self.ring.pos, h)[...] + self.landing[h, 0, last - 1] + self.landing[1 - h, 1, last - 2]
                for h in (0, 1)]


class AllGather:
    def __init__(self, ring, full, half):
        self.ring, self.full, self.half = ring, full, half
        self.kib = kib(full(ring.pos))
        self.half_ring = ring.size // 2
        self.slots = {t: ring.links.slot() for t in range(1, self.half_ring + 1)}

    def wait(self, t):
        self.ring.links.arrived(self.slots[t], 2 * self.kib if t < self.half_ring else self.kib)

    def step(self, t):
        if t > 1:
            self.wait(t - 1)
        for d, sign in ((0, -1), (1, 1)):
            owner = self.ring.at(-sign * (t - 1))
            src = self.half(owner, d) if t == self.half_ring else self.full(owner)
            self.ring.links.send(self.slots[t], src, src, self.ring.device(sign))
        return self.ring.links.clock.sent(self.ring.axis, self.kib if t < self.half_ring else self.kib / 2)

    def final(self):
        self.wait(self.half_ring)

    def flow(self, reached=None):
        for t in range(1, self.half_ring + 1):
            due = self.step(t)
            if reached is not None:
                reached(t - 1)
            yield due
        self.final()
        if reached is not None:
            reached(self.half_ring)


class Direct:
    def __init__(self, ring, source, target):
        links = self.links = ring.links
        order = sorted(range(1, ring.size), key=lambda d: -min(d, ring.size - d))
        self.slot, self.kib = links.slot(), kib(source(ring.pos))
        self.total = self.kib * len(order)
        for d in order:
            links.send(self.slot, source(ring.at(d)), target(ring.pos, d), ring.device(d))
        wide = ring.size > 4
        self.due = links.clock.sent(ring.axis, self.kib * (9 if wide else 3), 1.9 if wide else 2.6)

    def final(self):
        self.links.arrived(self.slot, self.total)


def summed_block(ring, own, landing, relay, direct):
    if not direct:
        halves = yield from ReduceScatter(ring, own, relay).flow()
        return halves
    whole = own(ring.pos, None)
    moved = Direct(ring, lambda o: own(o, None), lambda o, d: landing.at[d])
    yield moved.due
    moved.final()
    total = whole[...]
    for d in range(1, ring.size):
        total = total + landing[d]
    return [total[:8], total[8:]]


def gathered(ring, full, half, direct):
    if not direct:
        yield from AllGather(ring, full, half).flow()
    else:
        moved = Direct(ring, lambda o: full(ring.pos), lambda o, d: full(o))
        yield moved.due
        moved.final()


def rows8(h):
    return slice(None) if h is None else pl.ds(8 * h, 8)


def place():
    y, s, c = lax.axis_index("view"), lax.axis_index("sent"), lax.axis_index("col")
    return y, s // NZ, lax.rem(s, NZ), c


def rings(links, x, z, y):
    def x_dev(delta):
        return {"sent": lax.rem(x + (delta % NX), NX) * NZ + z}

    def z_dev(delta):
        return {"sent": x * NZ + lax.rem(z + (delta % NZ), NZ)}

    def y_dev(delta):
        return {"view": lax.rem(y + (delta % NY), NY)}

    return (Ring(links, "x", NX, x, x_dev), Ring(links, "z", NZ, z, z_dev), Ring(links, "y", NY, y, y_dev))


def nt(a, b):
    return lax.dot_general(a, b, (((1,), (1,)), ((), ())), precision=HIGH, preferred_element_type=F32)


def nn(a, b):
    return lax.dot_general(a, b, (((1,), (0,)), ((), ())), precision=HIGH, preferred_element_type=F32)


CHAINS = (
    (0, 0, 0.02, "z", "z", (True, False, True, True, True, False)),
    (0, 1, 1.01, "x", "z", (True, False, False, False, True, False)),
    (1, 0, 2.03, "x", "x", (False, True, True, True, False, True)),
    (1, 1, 2.05, "z", "z", (False, True, False, True, True, False)),
    (2, 0, 10.04, "z", "x", (True, True, True, True, True, True)),
    (2, 1, 11.0, "x", "x", (False, True, True, False, True, True)),
)
INV_START = 15.0


def project(scale, widths, shared, inv, sketched, loadings, merged_out, gram_out,
            feats, sharedH, sharedT, terms, land_x, land_xz, land_z, land_zx, quarter, slab, proj, invx, hop,
            part, part_in, part_sum, land_h, half, back, land_b, loadT, stage, merged, gram, land_8, land_4,
            contrib, mine_in, mine_sum, land_m, outer, outer_in, outer_sum, from_y, over_x, over_z,
            send_sems, recv_sems, feat_sems, own_sems, out_sems):
    y, x, z, c = place()
    links = Links(send_sems, recv_sems, stage)
    clock = links.clock
    rx, rz, ry = rings(links, x, z, y)
    partner = {"col": 1 - c}

    bring_shared = pltpu.make_async_copy(shared, sharedH, own_sems.at[0])
    bring_shared.start()
    barrier = pltpu.get_barrier_semaphore()
    peers = [partner] + [ring.device(d) for ring in (rx, rz, ry) for d in range(1, ring.size)]
    for peer in peers:
        pl.semaphore_signal(barrier, inc=1, device_id=peer, device_id_type=MESH)

    def columns(q):
        return pl.ds(pl.multiple_of(q * 256, 256), 256)

    quarters = [rx.at(d) for d in (2, 3, 1, 0)]
    loads = {}
    for v in range(3):
        for n, q in enumerate(quarters):
            loads[v, n] = pltpu.make_async_copy(sketched.at[v, :, columns(q)], feats.at[v, q], feat_sems.at[4 * v + n])
            loads[v, n].start()
    own_inv = pltpu.make_async_copy(inv.at[:, :, columns(x)], invx.at[:, x], own_sems.at[1])
    own_inv.start()
    bring_shared.wait()
    sharedT[...] = sharedH[...].T

    first_col = c * 1024 + x * 256
    lane = lax.broadcasted_iota(jnp.int32, (8, 256), 1)
    row = (lane // 64) * (64 * NZ) + z * 64 + lax.rem(lane, 64)

    def lanes_kept(v, value):
        return jnp.where(first_col + lane < widths[v], value, 0.0)

    inv_slots = {(v, kind): links.slot() for v in range(3) for kind in ("near", "hop", "far")}

    def inv_flow():
        for v in range(3):
            for i, sign in enumerate((1, -1)):
                links.send(inv_slots[v, "near"], inv.at[v, :, columns(rx.at(sign))], invx.at[v, x], rx.device(sign))
                links.send(inv_slots[v, "hop"], inv.at[v, pl.ds(32 * i, 32), columns(rx.at(2))],
                           hop.at[v, i], rx.device(sign))
            due = clock.sent("x", 96)
            yield clock.now
        yield due
        for v in range(3):
            links.arrived(inv_slots[v, "hop"], 64)
            for i, sign in enumerate((1, -1)):
                links.send(inv_slots[v, "far"], hop.at[v, i], invx.at[v, rx.at(-sign), pl.ds(32 * i, 32)],
                           rx.device(sign))
            due = clock.sent("x", 32)
            yield clock.now

    sending_inv = inv_flow()
    inv_here = set()

    def need_inv(v):
        for _ in sending_inv:
            pass
        if not inv_here:
            own_inv.wait()
        if v not in inv_here:
            inv_here.add(v)
            links.arrived(inv_slots[v, "near"], 128)
            links.arrived(inv_slots[v, "far"], 64)

    def swap(src, dst):
        slot = links.slot()
        links.send(slot, src, dst, partner)
        yield clock.now + 1.55
        links.arrived(slot, kib(src))

    used = []

    def use(v, k, q):
        block = loadT[v, k, q].reshape(128, 256).T
        stage[v, columns(q), 128 * k:128 * k + 128] = block
        product = jnp.dot(feats[v, q], block.astype(BF16), preferred_element_type=F32).reshape(2, NY, 128, 128)
        here = slice(128 * k, 128 * k + 128)
        contrib[:, :, :, here] = contrib[:, :, :, here] + product if k in used else product
        used.append(k)

    made = set()

    def make_terms(v):
        if v in made:
            return
        made.add(v)
        for n, q in enumerate(quarters):
            loads[v, n].wait()
            terms[v, :, q] = jnp.dot(sharedT[...], feats[v, q], preferred_element_type=F32).reshape(2, NZ, 16, 256)
        if len(made) == 1:
            pl.semaphore_wait(barrier, len(peers))

    def chain(v, k, first, last, direct):
        make_terms(v)
        if first == "x":
            halves = yield from ReduceScatter(
                rx, lambda o, h: terms.at[v, k, o, pl.ds(4 * h, 4)], land_x.at[v, k]).flow()
            for h in (0, 1):
                quarter[v, k, pl.ds(4 * h, 4)] = halves[h]
            halves = yield from summed_block(
                rz, lambda o, h: quarter.at[v, k, o, rows8(h)], land_8.at[v, k, 0], land_xz.at[v, k], direct[0])
        else:
            halves = yield from ReduceScatter(
                rz, lambda o, h: terms.at[v, k, :, o, pl.ds(8 * h, 8)], land_z.at[v, k]).flow()
            for h in (0, 1):
                slab[v, k, :, pl.ds(8 * h, 8)] = halves[h]
            halves = yield from summed_block(
                rx, lambda o, h: slab.at[v, k, o, rows8(h)], land_4.at[v, k, 0], land_zx.at[v, k], direct[0])
        for h in (0, 1):
            proj[v, k, z, pl.ds(8 * h, 8)] = lanes_kept(v, halves[h] * scale)
        yield from gathered(rz, lambda o: proj.at[v, k, o], lambda o, h: proj.at[v, k, o, rows8(h)], direct[1])

        need_inv(v)
        part[v, k] = nt(proj[v, k].reshape(128, 256), invx[v].reshape(256, 256)).reshape(2, NX, 16, 256)
        yield from swap(part.at[v, k, 1 - c], part_in.at[v, k])
        part_sum[v, k] = part[v, k, c] + part_in[v, k]
        halves = yield from summed_block(
            rx, lambda o, h: part_sum.at[v, k, o, rows8(h)], land_4.at[v, k, 1], land_h.at[v, k], direct[2])
        for h in (0, 1):
            half[v, k, c, x, pl.ds(8 * h, 8)] = jnp.where(row < widths[v], halves[h], 0.0)
        yield from gathered(rx, lambda o: half.at[v, k, c, o], lambda o, h: half.at[v, k, c, o, rows8(h)], direct[3])
        yield from swap(half.at[v, k, c], half.at[v, k, c])

        back[v, k] = nn(half[v, k].reshape(128, 256), invx[v].reshape(256, 256)).reshape(NZ, 16, 256)
        halves = yield from summed_block(
            rz, lambda o, h: back.at[v, k, o, rows8(h)], land_8.at[v, k, 1], land_b.at[v, k], direct[4])
        for h in (0, 1):
            loadT[v, k, x, z, pl.ds(8 * h, 8)] = lanes_kept(v, halves[h])
        if last == "x":
            yield from gathered(
                rx, lambda o: loadT.at[v, k, o, z], lambda o, h: loadT.at[v, k, o, z, rows8(h)], direct[5])
            yield from AllGather(
                rz, lambda o: loadT.at[v, k, :, o], lambda o, h: loadT.at[v, k, :, o, pl.ds(8 * h, 8)]).flow()
            for q in range(NX):
                use(v, k, q)
        else:
            yield from gathered(
                rz, lambda o: loadT.at[v, k, x, o], lambda o, h: loadT.at[v, k, x, o, rows8(h)], direct[5])

            def reached(t):
                for d in sorted({t % NX, -t % NX}):
                    use(v, k, rx.at(d))

            yield from AllGather(
                rx, lambda o: loadT.at[v, k, o], lambda o, h: loadT.at[v, k, o, pl.ds(4 * h, 4)]).flow(reached)

    for v, k, start, first, last, direct in CHAINS:
        clock.add(start, chain(v, k, first, last, direct))
    clock.add(INV_START, sending_inv)
    clock.run()
    put_loadings = pltpu.make_async_copy(stage, loadings, out_sems.at[0])
    put_loadings.start()

    slots = {d: links.slot() for d in (2, 1, 3, 0)}
    for d, slot in slots.items():
        links.send(slot, contrib.at[1 - c, ry.at(d)], mine_in.at[ry.at(d)], partner)

    def summed(d):
        o = ry.at(d)
        links.arrived(slots[d], 128)
        mine_sum[o] = contrib[c, o] + mine_in[o]

    ms = ReduceScatter(ry, lambda o, h: mine_sum.at[o, pl.ds(64 * h, 64)], land_m)
    summed(2)
    ms.step(1, 0)
    summed(1)
    summed(3)
    ms.step(1, 1)
    summed(0)
    ms.step(2, 0)
    halves = ms.final()
    for h in (0, 1):
        merged[c, y, pl.ds(64 * h, 64)] = halves[h]
    rows = merged[c, y]

    outer[...] = tn(rows, rows).reshape(2, NY, 32, 256)
    slot = links.slot()
    links.send(slot, outer.at[1 - c], outer_in, partner)
    links.arrived(slot, 128)
    outer_sum[...] = outer[c] + outer_in[...]
    gs = Direct(ry, lambda o: outer_sum.at[o], lambda o, d: from_y.at[o])
    mg = AllGather(ry, lambda o: merged.at[c, o], lambda o, h: merged.at[c, o, pl.ds(64 * h, 64)])
    from_y[y] = outer_sum[y]
    gs.final()
    mg.step(1)
    over_x[x] = (from_y[0] + from_y[1]) + (from_y[2] + from_y[3])
    Direct(rx, lambda o: over_x.at[x], lambda o, d: over_x.at[o]).final()
    over_z[z] = (over_x[0] + over_x[1]) + (over_x[2] + over_x[3])
    gz = Direct(rz, lambda o: over_z.at[z], lambda o, d: over_z.at[o])
    mg.step(2)
    mg.final()
    slot = links.slot()
    links.send(slot, merged.at[c], merged.at[c], partner)
    gz.final()
    acc = over_z[0]
    for i in range(1, NZ):
        acc = acc + over_z[i]
    gram[c, y] = acc
    gy = Direct(ry, lambda o: gram.at[c, y], lambda o, d: gram.at[c, o])
    links.arrived(slot, 512)
    put_merged = pltpu.make_async_copy(merged, merged_out, out_sems.at[1])
    put_merged.start()
    gy.final()
    last = links.slot()
    links.send(last, gram.at[c], gram.at[c], partner)
    links.arrived(last, 128)
    put_gram = pltpu.make_async_copy(gram, gram_out, out_sems.at[2])
    put_gram.start()
    put_loadings.wait()
    put_merged.wait()
    links.drain()
    put_gram.wait()


PANEL = 32


def panel_inverse(tiles, lane0):
    groups = PANEL // 8
    sub = lax.broadcasted_iota(jnp.int32, (8, 128), 0)
    lane = lax.broadcasted_iota(jnp.int32, (8, 128), 1)

    def spread(tile, s):
        return jnp.broadcast_to(tile[s:s + 1, :], (8, 128))

    cols = [{g: jnp.broadcast_to(tiles[g][:, lane0 + j:lane0 + j + 1], (8, 128)) for g in range(j // 8, groups)}
            for j in range(PANEL)]
    unit = [jnp.where(lane == sub + 8 * g, 1.0, 0.0).astype(F32) for g in range(groups)]
    pivots = [jnp.ones((8, 128), F32) for g in range(groups)]
    for k in range(PANEL):
        gk, sk = divmod(k, 8)
        pivot = spread(cols[k][gk], sk)
        inverse = 1.0 / pivot
        pivots[gk] = jnp.where(sub == sk, pivot, pivots[gk])
        mult = {g: cols[k][g] * inverse for g in range(gk, groups)}
        for j in range(k + 1, PANEL):
            gj, sj = divmod(j, 8)
            entry = spread(cols[k][gj], sj)
            for g in range(gj, groups):
                cols[j][g] = cols[j][g] - mult[g] * entry
        row = spread(unit[gk], sk)
        for g in range(gk, groups):
            m = jnp.where(sub > sk, mult[g], 0.0) if g == gk else mult[g]
            unit[g] = unit[g] - m * row
    return jnp.concatenate([unit[g] * lax.rsqrt(pivots[g]) for g in range(groups)], axis=0)[:, :PANEL]


def tn(a, b):
    return lax.dot_general(a, b, (((0,), (0,)), ((), ())), precision=HIGH, preferred_element_type=F32)


def factor_inverse(work, inverse, between):
    n = work.shape[0]
    for p in range(n // PANEL):
        r0 = p * PANEL
        lt = r0 // 128 * 128
        tiles = [work[r0 + 8 * g:r0 + 8 * g + 8, lt:lt + 128] for g in range(PANEL // 8)]
        block = panel_inverse(tiles, r0 - lt)
        col = lax.broadcasted_iota(jnp.int32, (PANEL, n), 1)
        row = lax.broadcasted_iota(jnp.int32, (PANEL, n), 0)
        here = (col >= r0) & (col < r0 + PANEL)
        wide = jnp.where(here, jnp.where(col == row + r0, 1.0, 0.0), work[r0:r0 + PANEL, :])
        u = nn(block, wide)
        inverse[r0:r0 + PANEL, :] = jnp.where(col < r0 + PANEL, u, 0.0)
        between(p)
        r1 = r0 + PANEL
        if r1 < n:
            base = r1 // 128 * 128
            upd = tn(u[:, base:], u)[r1 - base:]
            col = lax.broadcasted_iota(jnp.int32, (n - r1, n), 1)
            here = (col >= r0) & (col < r1)
            work[r1:, :] = jnp.where(here, 0.0, work[r1:, :]) - upd


def solve(root, gram, merged, loaded, updated, loadings, work, inverse, rows, passing, solved, sems):
    bring_gram = pltpu.make_async_copy(gram, work, sems.at[0])
    bring_rows = pltpu.make_async_copy(merged, rows, sems.at[1])
    bring = pltpu.make_async_copy(loaded, passing, sems.at[2])
    put = pltpu.make_async_copy(passing, loadings, sems.at[3])
    bring_gram.start()
    bring_rows.start()
    bring.start()
    bring_gram.wait()

    def between(panel):
        if panel == 2:
            bring.wait()
            put.start()

    factor_inverse(work, inverse, between)
    bring_rows.wait()
    puts = []
    for i in range(4):
        here = slice(256 * i, 256 * i + 256)
        solved[here, :] = nt(rows[here, :], inverse[...]) * root
        puts.append(pltpu.make_async_copy(solved.at[here], updated.at[here], sems.at[4 + i]))
        puts[-1].start()
    put.wait()
    for copy in puts:
        copy.wait()


def shards(sketched, widths, inv_factor, shared):
    total_rows = shared.shape[0] * lax.axis_size("sent")
    smem, hbm = (pl.BlockSpec(memory_space=m) for m in (pltpu.SMEM, pltpu.HBM))

    def buf(*shape):
        return pltpu.VMEM(shape, F32)

    sems = [pltpu.SemaphoreType.DMA((SEND_SEMS,)), pltpu.SemaphoreType.DMA((RECV_SEMS,))]

    def kernel_a(*refs):
        project(1.0 / math.sqrt(total_rows), *refs)

    loadings, merged, gram = pl.pallas_call(
        kernel_a,
        name="project",
        out_shape=(jax.ShapeDtypeStruct((3, 1024, 256), F32), jax.ShapeDtypeStruct((2, NY, 128, 256), F32),
                   jax.ShapeDtypeStruct((2, NY, 32, 256), F32)),
        in_specs=[smem, hbm, hbm, hbm],
        out_specs=(hbm, hbm, hbm),
        scratch_shapes=[
            pltpu.VMEM((3, 4, 1024, 256), BF16), pltpu.VMEM((1024, 256), BF16), pltpu.VMEM((256, 1024), BF16),
            buf(3, 2, 4, 8, 16, 256), buf(3, 2, 2, 2, 2, 4, 16, 256), buf(3, 2, 2, 2, 4, 8, 256),
            buf(3, 2, 2, 2, 4, 4, 8, 256), buf(3, 2, 2, 2, 2, 8, 256), buf(3, 2, 8, 16, 256), buf(3, 2, 4, 16, 256),
            buf(3, 2, 8, 16, 256), buf(3, 4, 64, 256), buf(3, 2, 32, 256),
            buf(3, 2, 2, 4, 16, 256), buf(3, 2, 4, 16, 256), buf(3, 2, 4, 16, 256), buf(3, 2, 2, 2, 2, 8, 256),
            buf(3, 2, 2, 4, 16, 256), buf(3, 2, 8, 16, 256), buf(3, 2, 2, 2, 4, 8, 256), buf(3, 2, 4, 8, 16, 256),
            buf(3, 1024, 256), buf(2, NY, 128, 256), buf(2, NY, 32, 256), buf(3, 2, 2, 8, 16, 256), buf(3, 2, 2, 4, 16, 256),
            buf(2, 4, 128, 256), buf(4, 128, 256), buf(4, 128, 256), buf(2, 2, 2, 64, 256), buf(2, 4, 32, 256),
            buf(4, 32, 256), buf(4, 32, 256), buf(4, 32, 256), buf(4, 32, 256), buf(8, 32, 256), *sems,
            pltpu.SemaphoreType.DMA((12,)), pltpu.SemaphoreType.DMA((2,)), pltpu.SemaphoreType.DMA((3,))],
        compiler_params=pltpu.CompilerParams(collective_id=0, has_side_effects=True, vmem_limit_bytes=58 * 2**20),
    )(widths, shared, inv_factor, sketched)
    merged, gram = merged.reshape(1024, 256), gram.reshape(256, 256)

    def kernel_c(*refs):
        solve(math.sqrt(total_rows), *refs)

    updated, loadings = pl.pallas_call(
        kernel_c,
        name="solve",
        out_shape=(jax.ShapeDtypeStruct((1024, 256), F32), jax.ShapeDtypeStruct((3, 1024, 256), F32)),
        in_specs=[hbm, hbm, hbm],
        out_specs=(hbm, hbm),
        scratch_shapes=[buf(256, 256), buf(256, 256), buf(1024, 256), buf(3, 1024, 256), buf(1024, 256),
                        pltpu.SemaphoreType.DMA((8,))],
        compiler_params=pltpu.CompilerParams(vmem_limit_bytes=58 * 2**20),
    )(gram, merged, loadings)
    return (loadings, updated)


def solution(mesh):
    return jax.shard_map(
        shards,
        mesh=mesh,
        in_specs=(P("view", "sent", "col"), P("view"), P("view", "sent", "col"), P("sent", None)),
        out_specs=(P("view", "col", None), P("sent", None)),
        check_vma=False,
    )
```

```python
import math

import jax
import jax.numpy as jnp
from jax import lax
from jax.experimental import pallas as pl
from jax.experimental.pallas import tpu as pltpu
from jax.sharding import PartitionSpec as P

MESH = pl.DeviceIdType.MESH
HIGH = lax.Precision.HIGHEST
F32 = jnp.float32
BF16 = jnp.bfloat16
NX, NZ, NY = 4, 8, 4
SEND_SEMS, RECV_SEMS = 40, 224


class Clock:
    def __init__(self):
        self.now, self.busy, self.flows = 0.0, {}, []

    def sent(self, axis, kib, latency=2.4):
        self.busy[axis] = max(self.now, self.busy.get(axis, 0.0)) + kib * 0.0225
        return self.busy[axis] + latency

    def add(self, start, flow):
        self.flows.append([start, len(self.flows), flow])

    def run(self):
        while self.flows:
            item = min(self.flows)
            self.now = max(self.now, item[0]) + 0.1
            try:
                item[0] = next(item[2])
            except StopIteration:
                self.flows.remove(item)


def kib(ref):
    return math.prod(ref.shape) * 4 // 1024


class Links:
    def __init__(self, send_sems, recv_sems, ruler):
        self.send_sems, self.recv_sems, self.ruler = send_sems, recv_sems, ruler
        self.used, self.groups, self.clock = 0, [], Clock()

    def slot(self):
        self.used += 1
        assert self.used <= RECV_SEMS
        return self.used - 1

    def send(self, slot, src, dst, device):
        size = kib(src)
        if not self.groups or self.groups[-1] + size > 1024:
            self.groups.append(0)
            assert len(self.groups) <= SEND_SEMS
        self.groups[-1] += size
        pltpu.make_async_remote_copy(
            src_ref=src, dst_ref=dst, send_sem=self.send_sems.at[len(self.groups) - 1],
            recv_sem=self.recv_sems.at[slot], device_id=device, device_id_type=MESH).start()

    def wait(self, sem, size):
        rows = self.ruler.at[0, pl.ds(0, size)]
        pltpu.make_async_copy(rows, rows, sem).wait()

    def arrived(self, slot, size):
        self.wait(self.recv_sems.at[slot], size)

    def drain(self):
        for group, size in enumerate(self.groups):
            self.wait(self.send_sems.at[group], size)


class Ring:
    def __init__(self, links, axis, size, pos, device):
        self.links, self.axis, self.size, self.pos, self.device = links, axis, size, pos, device

    def at(self, delta):
        return lax.rem(self.pos + (delta % self.size), self.size)


class ReduceScatter:
    def __init__(self, ring, own, landing):
        self.ring, self.own, self.landing = ring, own, landing
        self.kib = kib(landing.at[0, 0, 0])
        self.half_ring = ring.size // 2
        self.slots = {(kind, t): ring.links.slot()
                      for t in range(1, self.half_ring + 1) for kind in (0, 1)
                      if not (kind == 1 and t == self.half_ring)}

    def wait(self, kind, t):
        self.ring.links.arrived(self.slots[kind, t], 2 * self.kib)

    def step(self, t, kind):
        if t > 1:
            self.wait(kind, t - 1)
        for d, sign in ((0, -1), (1, 1)):
            dist = self.half_ring + 1 - t - kind
            src = self.own(self.ring.at(sign * dist), d if kind == 0 else 1 - d)
            if t > 1:
                buf = self.landing.at[d, kind, t - 2]
                buf[...] = buf[...] + src[...]
                src = buf
            self.ring.links.send(self.slots[kind, t], src, self.landing.at[d, kind, t - 1], self.ring.device(sign))
        return self.ring.links.clock.sent(self.ring.axis, self.kib)

    def flow(self):
        due = {}
        for t in range(1, self.half_ring + 1):
            for kind in (0, 1):
                if (kind, t) not in self.slots:
                    continue
                if t > 1:
                    yield due[kind]
                due[kind] = self.step(t, kind)
        yield max(due.values())
        return self.final()

    def final(self):
        last = self.half_ring
        self.wait(0, last)
        self.wait(1, last - 1)
        return [self.own(self.ring.pos, h)[...] + self.landing[h, 0, last - 1] + self.landing[1 - h, 1, last - 2]
                for h in (0, 1)]


class AllGather:
    def __init__(self, ring, full, half):
        self.ring, self.full, self.half = ring, full, half
        self.kib = kib(full(ring.pos))
        self.half_ring = ring.size // 2
        self.slots = {t: ring.links.slot() for t in range(1, self.half_ring + 1)}

    def wait(self, t):
        self.ring.links.arrived(self.slots[t], 2 * self.kib if t < self.half_ring else self.kib)

    def step(self, t):
        if t > 1:
            self.wait(t - 1)
        for d, sign in ((0, -1), (1, 1)):
            owner = self.ring.at(-sign * (t - 1))
            src = self.half(owner, d) if t == self.half_ring else self.full(owner)
            self.ring.links.send(self.slots[t], src, src, self.ring.device(sign))
        return self.ring.links.clock.sent(self.ring.axis, self.kib if t < self.half_ring else self.kib / 2)

    def final(self):
        self.wait(self.half_ring)

    def flow(self, reached=None):
        for t in range(1, self.half_ring + 1):
            due = self.step(t)
            if reached is not None:
                reached(t - 1)
            yield due
        self.final()
        if reached is not None:
            reached(self.half_ring)


class Direct:
    def __init__(self, ring, source, target):
        links = self.links = ring.links
        order = sorted(range(1, ring.size), key=lambda d: -min(d, ring.size - d))
        self.slot, self.kib = links.slot(), kib(source(ring.pos))
        self.total = self.kib * len(order)
        for d in order:
            links.send(self.slot, source(ring.at(d)), target(ring.pos, d), ring.device(d))
        wide = ring.size > 4
        self.due = links.clock.sent(ring.axis, self.kib * (9 if wide else 3), 1.9 if wide else 2.6)

    def final(self):
        self.links.arrived(self.slot, self.total)


def summed_block(ring, own, landing, relay, direct):
    if not direct:
        halves = yield from ReduceScatter(ring, own, relay).flow()
        return halves
    whole = own(ring.pos, None)
    moved = Direct(ring, lambda o: own(o, None), lambda o, d: landing.at[d])
    yield moved.due
    moved.final()
    total = whole[...]
    for d in range(1, ring.size):
        total = total + landing[d]
    return [total[:8], total[8:]]


def gathered(ring, full, half, direct):
    if not direct:
        yield from AllGather(ring, full, half).flow()
    else:
        moved = Direct(ring, lambda o: full(ring.pos), lambda o, d: full(o))
        yield moved.due
        moved.final()


def rows8(h):
    return slice(None) if h is None else pl.ds(8 * h, 8)


def place():
    y, s, c = lax.axis_index("view"), lax.axis_index("sent"), lax.axis_index("col")
    return y, s // NZ, lax.rem(s, NZ), c


def rings(links, x, z, y):
    def x_dev(delta):
        return {"sent": lax.rem(x + (delta % NX), NX) * NZ + z}

    def z_dev(delta):
        return {"sent": x * NZ + lax.rem(z + (delta % NZ), NZ)}

    def y_dev(delta):
        return {"view": lax.rem(y + (delta % NY), NY)}

    return (Ring(links, "x", NX, x, x_dev), Ring(links, "z", NZ, z, z_dev), Ring(links, "y", NY, y, y_dev))


def nt(a, b):
    return lax.dot_general(a, b, (((1,), (1,)), ((), ())), precision=HIGH, preferred_element_type=F32)


def nn(a, b):
    return lax.dot_general(a, b, (((1,), (0,)), ((), ())), precision=HIGH, preferred_element_type=F32)


CHAINS = (
    (0, 0, 0.0, "z", "z", (True, True, True, True, True, False)),
    (0, 1, 0.03, "x", "z", (False, True, True, True, True, False)),
    (1, 0, 1.02, "x", "x", (False, True, True, True, True, True)),
    (1, 1, 1.05, "z", "x", (True, False, True, True, True, True)),
    (2, 0, 2.04, "z", "z", (True, True, True, True, True, False)),
    (2, 1, 10.01, "z", "x", (True, True, True, True, True, True)),
)
INV_START = 12.0


def project(scale, widths, shared, inv, sketched, loadings, merged_out, gram_out,
            feats, sharedH, sharedT, terms, land_x, land_xz, land_z, land_zx, quarter, slab, proj, invx, hop,
            part, part_in, part_sum, land_h, half, back, land_b, loadT, stage, merged, gram, land_8, land_4,
            contrib, mine_in, mine_sum, land_m, outer, outer_in, outer_sum, from_y, sum_y, over_x, over_z,
            send_sems, recv_sems, feat_sems, own_sems, out_sems):
    y, x, z, c = place()
    links = Links(send_sems, recv_sems, stage)
    clock = links.clock
    rx, rz, ry = rings(links, x, z, y)
    partner = {"col": 1 - c}

    bring_shared = pltpu.make_async_copy(shared, sharedH, own_sems.at[0])
    bring_shared.start()
    barrier = pltpu.get_barrier_semaphore()
    peers = [partner] + [ring.device(d) for ring in (rx, rz, ry) for d in range(1, ring.size)]
    for peer in peers:
        pl.semaphore_signal(barrier, inc=1, device_id=peer, device_id_type=MESH)

    def columns(q):
        return pl.ds(pl.multiple_of(q * 256, 256), 256)

    quarters = [rx.at(d) for d in (2, 3, 1, 0)]
    loads = {}
    for v in range(3):
        for n, q in enumerate(quarters):
            loads[v, n] = pltpu.make_async_copy(sketched.at[v, :, columns(q)], feats.at[v, q], feat_sems.at[4 * v + n])
            loads[v, n].start()
    own_inv = pltpu.make_async_copy(inv.at[:, :, columns(x)], invx.at[:, x], own_sems.at[1])
    own_inv.start()
    bring_shared.wait()
    sharedT[...] = sharedH[...].T

    first_col = c * 1024 + x * 256
    lane = lax.broadcasted_iota(jnp.int32, (8, 256), 1)
    row = (lane // 64) * (64 * NZ) + z * 64 + lax.rem(lane, 64)

    def lanes_kept(v, value):
        return jnp.where(first_col + lane < widths[v], value, 0.0)

    inv_slots = {(v, kind): links.slot() for v in range(3) for kind in ("near", "hop", "far")}

    def inv_flow():
        for v in range(3):
            for i, sign in enumerate((1, -1)):
                links.send(inv_slots[v, "near"], inv.at[v, :, columns(rx.at(sign))], invx.at[v, x], rx.device(sign))
                links.send(inv_slots[v, "hop"], inv.at[v, pl.ds(32 * i, 32), columns(rx.at(2))],
                           hop.at[v, i], rx.device(sign))
            due = clock.sent("x", 96)
            yield clock.now
        yield due
        for v in range(3):
            links.arrived(inv_slots[v, "hop"], 64)
            for i, sign in enumerate((1, -1)):
                links.send(inv_slots[v, "far"], hop.at[v, i], invx.at[v, rx.at(-sign), pl.ds(32 * i, 32)],
                           rx.device(sign))
            due = clock.sent("x", 32)
            yield clock.now

    sending_inv = inv_flow()
    inv_here = set()

    def need_inv(v):
        for _ in sending_inv:
            pass
        if not inv_here:
            own_inv.wait()
        if v not in inv_here:
            inv_here.add(v)
            links.arrived(inv_slots[v, "near"], 128)
            links.arrived(inv_slots[v, "far"], 64)

    def swap(src, dst):
        slot = links.slot()
        links.send(slot, src, dst, partner)
        yield clock.now + 1.55
        links.arrived(slot, kib(src))

    used = []

    def use(v, k, q):
        block = loadT[v, k, q].reshape(128, 256).T
        stage[v, columns(q), 128 * k:128 * k + 128] = block
        product = jnp.dot(feats[v, q], block.astype(BF16), preferred_element_type=F32).reshape(2, NY, 128, 128)
        here = slice(128 * k, 128 * k + 128)
        contrib[:, :, :, here] = contrib[:, :, :, here] + product if k in used else product
        used.append(k)

    made = set()

    def make_terms(v):
        if v in made:
            return
        made.add(v)
        for n, q in enumerate(quarters):
            loads[v, n].wait()
            terms[v, :, q] = jnp.dot(sharedT[...], feats[v, q], preferred_element_type=F32).reshape(2, NZ, 16, 256)
        if len(made) == 1:
            pl.semaphore_wait(barrier, len(peers))

    def chain(v, k, first, last, direct):
        make_terms(v)
        if first == "x":
            halves = yield from ReduceScatter(
                rx, lambda o, h: terms.at[v, k, o, pl.ds(4 * h, 4)], land_x.at[v, k]).flow()
            for h in (0, 1):
                quarter[v, k, pl.ds(4 * h, 4)] = halves[h]
            halves = yield from summed_block(
                rz, lambda o, h: quarter.at[v, k, o, rows8(h)], land_8.at[v, k, 0], land_xz.at[v, k], direct[0])
        else:
            halves = yield from ReduceScatter(
                rz, lambda o, h: terms.at[v, k, :, o, pl.ds(8 * h, 8)], land_z.at[v, k]).flow()
            for h in (0, 1):
                slab[v, k, :, pl.ds(8 * h, 8)] = halves[h]
            halves = yield from summed_block(
                rx, lambda o, h: slab.at[v, k, o, rows8(h)], land_4.at[v, k, 0], land_zx.at[v, k], direct[0])
        for h in (0, 1):
            proj[v, k, z, pl.ds(8 * h, 8)] = lanes_kept(v, halves[h] * scale)
        yield from gathered(rz, lambda o: proj.at[v, k, o], lambda o, h: proj.at[v, k, o, rows8(h)], direct[1])

        need_inv(v)
        part[v, k] = nt(proj[v, k].reshape(128, 256), invx[v].reshape(256, 256)).reshape(2, NX, 16, 256)
        yield from swap(part.at[v, k, 1 - c], part_in.at[v, k])
        part_sum[v, k] = part[v, k, c] + part_in[v, k]
        halves = yield from summed_block(
            rx, lambda o, h: part_sum.at[v, k, o, rows8(h)], land_4.at[v, k, 1], land_h.at[v, k], direct[2])
        for h in (0, 1):
            half[v, k, c, x, pl.ds(8 * h, 8)] = jnp.where(row < widths[v], halves[h], 0.0)
        yield from gathered(rx, lambda o: half.at[v, k, c, o], lambda o, h: half.at[v, k, c, o, rows8(h)], direct[3])
        yield from swap(half.at[v, k, c], half.at[v, k, c])

        back[v, k] = nn(half[v, k].reshape(128, 256), invx[v].reshape(256, 256)).reshape(NZ, 16, 256)
        halves = yield from summed_block(
            rz, lambda o, h: back.at[v, k, o, rows8(h)], land_8.at[v, k, 1], land_b.at[v, k], direct[4])
        for h in (0, 1):
            loadT[v, k, x, z, pl.ds(8 * h, 8)] = lanes_kept(v, halves[h])
        if last == "x":
            yield from gathered(
                rx, lambda o: loadT.at[v, k, o, z], lambda o, h: loadT.at[v, k, o, z, rows8(h)], direct[5])
            yield from AllGather(
                rz, lambda o: loadT.at[v, k, :, o], lambda o, h: loadT.at[v, k, :, o, pl.ds(8 * h, 8)]).flow()
            for q in range(NX):
                use(v, k, q)
        else:
            yield from gathered(
                rz, lambda o: loadT.at[v, k, x, o], lambda o, h: loadT.at[v, k, x, o, rows8(h)], direct[5])

            def reached(t):
                for d in sorted({t % NX, -t % NX}):
                    use(v, k, rx.at(d))

            yield from AllGather(
                rx, lambda o: loadT.at[v, k, o], lambda o, h: loadT.at[v, k, o, pl.ds(4 * h, 4)]).flow(reached)

    for v, k, start, first, last, direct in CHAINS:
        clock.add(start, chain(v, k, first, last, direct))
    clock.add(INV_START, sending_inv)
    clock.run()
    put_loadings = pltpu.make_async_copy(stage, loadings, out_sems.at[0])
    put_loadings.start()

    slots = {d: links.slot() for d in (2, 1, 3, 0)}
    for d, slot in slots.items():
        links.send(slot, contrib.at[1 - c, ry.at(d)], mine_in.at[ry.at(d)], partner)

    def summed(d):
        o = ry.at(d)
        links.arrived(slots[d], 128)
        mine_sum[o] = contrib[c, o] + mine_in[o]

    ms = ReduceScatter(ry, lambda o, h: mine_sum.at[o, pl.ds(64 * h, 64)], land_m)
    summed(2)
    ms.step(1, 0)
    summed(1)
    summed(3)
    ms.step(1, 1)
    summed(0)
    ms.step(2, 0)
    halves = ms.final()
    for h in (0, 1):
        merged[c, y, pl.ds(64 * h, 64)] = halves[h]
    rows = merged[c, y]

    outer[...] = tn(rows, rows).reshape(2, NY, 32, 256)
    slot = links.slot()
    links.send(slot, outer.at[1 - c], outer_in, partner)
    links.arrived(slot, 128)
    outer_sum[...] = outer[c] + outer_in[...]
    gs = Direct(ry, lambda o: outer_sum.at[o], lambda o, d: from_y.at[o])
    mg = AllGather(ry, lambda o: merged.at[c, o], lambda o, h: merged.at[c, o, pl.ds(64 * h, 64)])
    from_y[y] = outer_sum[y]
    gs.final()
    mg.step(1)
    sum_y[...] = ((from_y[0] + from_y[1]) + (from_y[2] + from_y[3])).reshape(NX, 8, 256)
    over_x[x] = sum_y[x]
    Direct(rx, lambda o: sum_y.at[o], lambda o, d: over_x.at[o]).final()
    over_z[z] = (over_x[0] + over_x[1]) + (over_x[2] + over_x[3])
    gz = Direct(rz, lambda o: over_z.at[z], lambda o, d: over_z.at[o])
    mg.step(2)
    gz.final()
    acc = over_z[0]
    for i in range(1, NZ):
        acc = acc + over_z[i]
    gram[c, y, x] = acc
    gx = Direct(rx, lambda o: gram.at[c, y, x], lambda o, d: gram.at[c, y, o])
    mg.final()
    slot = links.slot()
    links.send(slot, merged.at[c], merged.at[c], partner)
    gx.final()
    gy = Direct(ry, lambda o: gram.at[c, y], lambda o, d: gram.at[c, o])
    links.arrived(slot, 512)
    put_merged = pltpu.make_async_copy(merged, merged_out, out_sems.at[1])
    put_merged.start()
    gy.final()
    last = links.slot()
    links.send(last, gram.at[c], gram.at[c], partner)
    links.arrived(last, 128)
    put_gram = pltpu.make_async_copy(gram, gram_out, out_sems.at[2])
    put_gram.start()
    put_loadings.wait()
    put_merged.wait()
    links.drain()
    put_gram.wait()


PANEL = 32


def panel_inverse(tiles, lane0):
    groups = PANEL // 8
    sub = lax.broadcasted_iota(jnp.int32, (8, 128), 0)
    lane = lax.broadcasted_iota(jnp.int32, (8, 128), 1)

    def spread(tile, s):
        return jnp.broadcast_to(tile[s:s + 1, :], (8, 128))

    cols = [{g: jnp.broadcast_to(tiles[g][:, lane0 + j:lane0 + j + 1], (8, 128)) for g in range(j // 8, groups)}
            for j in range(PANEL)]
    unit = [jnp.where(lane == sub + 8 * g, 1.0, 0.0).astype(F32) for g in range(groups)]
    pivots = [jnp.ones((8, 128), F32) for g in range(groups)]
    for k in range(PANEL):
        gk, sk = divmod(k, 8)
        pivot = spread(cols[k][gk], sk)
        inverse = 1.0 / pivot
        pivots[gk] = jnp.where(sub == sk, pivot, pivots[gk])
        mult = {g: cols[k][g] * inverse for g in range(gk, groups)}
        for j in range(k + 1, PANEL):
            gj, sj = divmod(j, 8)
            entry = spread(cols[k][gj], sj)
            for g in range(gj, groups):
                cols[j][g] = cols[j][g] - mult[g] * entry
        row = spread(unit[gk], sk)
        for g in range(gk, groups):
            m = jnp.where(sub > sk, mult[g], 0.0) if g == gk else mult[g]
            unit[g] = unit[g] - m * row
    return jnp.concatenate([unit[g] * lax.rsqrt(pivots[g]) for g in range(groups)], axis=0)[:, :PANEL]


def tn(a, b):
    return lax.dot_general(a, b, (((0,), (0,)), ((), ())), precision=HIGH, preferred_element_type=F32)


def factor_inverse(work, inverse, between):
    n = work.shape[0]
    for p in range(n // PANEL):
        r0 = p * PANEL
        lt = r0 // 128 * 128
        tiles = [work[r0 + 8 * g:r0 + 8 * g + 8, lt:lt + 128] for g in range(PANEL // 8)]
        block = panel_inverse(tiles, r0 - lt)
        col = lax.broadcasted_iota(jnp.int32, (PANEL, n), 1)
        row = lax.broadcasted_iota(jnp.int32, (PANEL, n), 0)
        here = (col >= r0) & (col < r0 + PANEL)
        wide = jnp.where(here, jnp.where(col == row + r0, 1.0, 0.0), work[r0:r0 + PANEL, :])
        u = nn(block, wide)
        inverse[r0:r0 + PANEL, :] = jnp.where(col < r0 + PANEL, u, 0.0)
        between(p)
        r1 = r0 + PANEL
        if r1 < n:
            base = r1 // 128 * 128
            upd = tn(u[:, base:], u)[r1 - base:]
            col = lax.broadcasted_iota(jnp.int32, (n - r1, n), 1)
            here = (col >= r0) & (col < r1)
            work[r1:, :] = jnp.where(here, 0.0, work[r1:, :]) - upd


def solve(root, gram, merged, loaded, updated, loadings, work, inverse, rows, passing, solved, sems):
    bring_gram = pltpu.make_async_copy(gram, work, sems.at[0])
    bring_rows = pltpu.make_async_copy(merged, rows, sems.at[1])
    bring = pltpu.make_async_copy(loaded, passing, sems.at[2])
    put = pltpu.make_async_copy(passing, loadings, sems.at[3])
    bring_gram.start()
    bring_rows.start()
    bring.start()
    bring_gram.wait()

    def between(panel):
        if panel == 2:
            bring.wait()
            put.start()

    factor_inverse(work, inverse, between)
    bring_rows.wait()
    puts = []
    for i in range(4):
        here = slice(256 * i, 256 * i + 256)
        solved[here, :] = nt(rows[here, :], inverse[...]) * root
        puts.append(pltpu.make_async_copy(solved.at[here], updated.at[here], sems.at[4 + i]))
        puts[-1].start()
    put.wait()
    for copy in puts:
        copy.wait()


def shards(sketched, widths, inv_factor, shared):
    total_rows = shared.shape[0] * lax.axis_size("sent")
    smem, hbm = (pl.BlockSpec(memory_space=m) for m in (pltpu.SMEM, pltpu.HBM))

    def buf(*shape):
        return pltpu.VMEM(shape, F32)

    sems = [pltpu.SemaphoreType.DMA((SEND_SEMS,)), pltpu.SemaphoreType.DMA((RECV_SEMS,))]

    def kernel_a(*refs):
        project(1.0 / math.sqrt(total_rows), *refs)

    loadings, merged, gram = pl.pallas_call(
        kernel_a,
        name="project",
        out_shape=(jax.ShapeDtypeStruct((3, 1024, 256), F32), jax.ShapeDtypeStruct((2, NY, 128, 256), F32),
                   jax.ShapeDtypeStruct((2, NY, NX, 8, 256), F32)),
        in_specs=[smem, hbm, hbm, hbm],
        out_specs=(hbm, hbm, hbm),
        scratch_shapes=[
            pltpu.VMEM((3, 4, 1024, 256), BF16), pltpu.VMEM((1024, 256), BF16), pltpu.VMEM((256, 1024), BF16),
            buf(3, 2, 4, 8, 16, 256), buf(3, 2, 2, 2, 2, 4, 16, 256), buf(3, 2, 2, 2, 4, 8, 256),
            buf(3, 2, 2, 2, 4, 4, 8, 256), buf(3, 2, 2, 2, 2, 8, 256), buf(3, 2, 8, 16, 256), buf(3, 2, 4, 16, 256),
            buf(3, 2, 8, 16, 256), buf(3, 4, 64, 256), buf(3, 2, 32, 256),
            buf(3, 2, 2, 4, 16, 256), buf(3, 2, 4, 16, 256), buf(3, 2, 4, 16, 256), buf(3, 2, 2, 2, 2, 8, 256),
            buf(3, 2, 2, 4, 16, 256), buf(3, 2, 8, 16, 256), buf(3, 2, 2, 2, 4, 8, 256), buf(3, 2, 4, 8, 16, 256),
            buf(3, 1024, 256), buf(2, NY, 128, 256), buf(2, NY, NX, 8, 256), buf(3, 2, 2, 8, 16, 256), buf(3, 2, 2, 4, 16, 256),
            buf(2, 4, 128, 256), buf(4, 128, 256), buf(4, 128, 256), buf(2, 2, 2, 64, 256), buf(2, 4, 32, 256),
            buf(4, 32, 256), buf(4, 32, 256), buf(4, 32, 256), buf(4, 8, 256), buf(4, 8, 256), buf(8, 8, 256), *sems,
            pltpu.SemaphoreType.DMA((12,)), pltpu.SemaphoreType.DMA((2,)), pltpu.SemaphoreType.DMA((3,))],
        compiler_params=pltpu.CompilerParams(collective_id=0, has_side_effects=True, vmem_limit_bytes=58 * 2**20),
    )(widths, shared, inv_factor, sketched)
    merged, gram = merged.reshape(1024, 256), gram.reshape(256, 256)

    def kernel_c(*refs):
        solve(math.sqrt(total_rows), *refs)

    updated, loadings = pl.pallas_call(
        kernel_c,
        name="solve",
        out_shape=(jax.ShapeDtypeStruct((1024, 256), F32), jax.ShapeDtypeStruct((3, 1024, 256), F32)),
        in_specs=[hbm, hbm, hbm],
        out_specs=(hbm, hbm),
        scratch_shapes=[buf(256, 256), buf(256, 256), buf(1024, 256), buf(3, 1024, 256), buf(1024, 256),
                        pltpu.SemaphoreType.DMA((8,))],
        compiler_params=pltpu.CompilerParams(vmem_limit_bytes=58 * 2**20),
    )(gram, merged, loadings)
    return (loadings, updated)


def solution(mesh):
    return jax.shard_map(
        shards,
        mesh=mesh,
        in_specs=(P("view", "sent", "col"), P("view"), P("view", "sent", "col"), P("sent", None)),
        out_specs=(P("view", "col", None), P("sent", None)),
        check_vma=False,
    )
```

```python
import math

import jax
import jax.numpy as jnp
from jax import lax
from jax.experimental import pallas as pl
from jax.experimental.pallas import tpu as pltpu
from jax.sharding import PartitionSpec as P

MESH = pl.DeviceIdType.MESH
HIGH = lax.Precision.HIGHEST
F32 = jnp.float32
BF16 = jnp.bfloat16
NX, NZ, NY = 4, 8, 4
SEND_SEMS, RECV_SEMS = 12, 157


class Clock:
    def __init__(self):
        self.now, self.busy, self.flows = 0.0, {}, []

    def sent(self, axis, kib, latency=3.0):
        self.busy[axis] = max(self.now, self.busy.get(axis, 0.0)) + kib * 0.0225
        return self.busy[axis] + latency

    def add(self, start, flow):
        self.flows.append([start, len(self.flows), flow])

    def run(self):
        while self.flows:
            item = min(self.flows)
            self.now = max(self.now, item[0]) + 0.1
            try:
                item[0] = next(item[2])
            except StopIteration:
                self.flows.remove(item)


def kib(ref):
    return math.prod(ref.shape) * 4 // 1024


class Links:
    def __init__(self, send_sems, recv_sems, ruler):
        self.send_sems, self.recv_sems, self.ruler = send_sems, recv_sems, ruler
        self.used, self.groups, self.clock = 0, [], Clock()

    def slot(self):
        self.used += 1
        assert self.used <= RECV_SEMS
        return self.used - 1

    def send(self, slot, src, dst, device):
        size = kib(src)
        if not self.groups or self.groups[-1] + size > 1024:
            self.groups.append(0)
            assert len(self.groups) <= SEND_SEMS
        self.groups[-1] += size
        pltpu.make_async_remote_copy(
            src_ref=src, dst_ref=dst, send_sem=self.send_sems.at[len(self.groups) - 1],
            recv_sem=self.recv_sems.at[slot], device_id=device, device_id_type=MESH).start()

    def wait(self, sem, size):
        rows = self.ruler.at[0, pl.ds(0, size)]
        pltpu.make_async_copy(rows, rows, sem).wait()

    def arrived(self, slot, size):
        self.wait(self.recv_sems.at[slot], size)

    def drain(self):
        for group, size in enumerate(self.groups):
            self.wait(self.send_sems.at[group], size)


class Ring:
    def __init__(self, links, axis, size, pos, device):
        self.links, self.axis, self.size, self.pos, self.device = links, axis, size, pos, device

    def at(self, delta):
        return lax.rem(self.pos + (delta % self.size), self.size)


class ReduceScatter:
    def __init__(self, ring, own, landing):
        self.ring, self.own, self.landing = ring, own, landing
        self.kib = kib(landing.at[0, 0, 0])
        self.half_ring = ring.size // 2
        self.slots = {(kind, t): ring.links.slot()
                      for t in range(1, self.half_ring + 1) for kind in (0, 1)
                      if not (kind == 1 and t == self.half_ring)}

    def wait(self, kind, t):
        self.ring.links.arrived(self.slots[kind, t], 2 * self.kib)

    def step(self, t, kind):
        if t > 1:
            self.wait(kind, t - 1)
        for d, sign in ((0, -1), (1, 1)):
            dist = self.half_ring + 1 - t - kind
            src = self.own(self.ring.at(sign * dist), d if kind == 0 else 1 - d)
            if t > 1:
                buf = self.landing.at[d, kind, t - 2]
                buf[...] = buf[...] + src[...]
                src = buf
            self.ring.links.send(self.slots[kind, t], src, self.landing.at[d, kind, t - 1], self.ring.device(sign))
        return self.ring.links.clock.sent(self.ring.axis, self.kib)

    def flow(self):
        due = {}
        for t in range(1, self.half_ring + 1):
            for kind in (0, 1):
                if (kind, t) not in self.slots:
                    continue
                if t > 1:
                    yield due[kind]
                due[kind] = self.step(t, kind)
        yield max(due.values())
        return self.final()

    def final(self):
        last = self.half_ring
        self.wait(0, last)
        self.wait(1, last - 1)
        return [self.own(self.ring.pos, h)[...] + self.landing[h, 0, last - 1] + self.landing[1 - h, 1, last - 2]
                for h in (0, 1)]


class AllGather:
    def __init__(self, ring, full, half):
        self.ring, self.full, self.half = ring, full, half
        self.kib = kib(full(ring.pos))
        self.half_ring = ring.size // 2
        self.slots = {t: ring.links.slot() for t in range(1, self.half_ring + 1)}

    def wait(self, t):
        self.ring.links.arrived(self.slots[t], 2 * self.kib if t < self.half_ring else self.kib)

    def step(self, t):
        if t > 1:
            self.wait(t - 1)
        for d, sign in ((0, -1), (1, 1)):
            owner = self.ring.at(-sign * (t - 1))
            src = self.half(owner, d) if t == self.half_ring else self.full(owner)
            self.ring.links.send(self.slots[t], src, src, self.ring.device(sign))
        return self.ring.links.clock.sent(self.ring.axis, self.kib if t < self.half_ring else self.kib / 2)

    def final(self):
        self.wait(self.half_ring)

    def flow(self, reached=None):
        for t in range(1, self.half_ring + 1):
            due = self.step(t)
            if reached is not None:
                reached(t - 1)
            yield due
        self.final()
        if reached is not None:
            reached(self.half_ring)


class Direct:
    def __init__(self, ring, source, target):
        links = self.links = ring.links
        order = sorted(range(1, ring.size), key=lambda d: -min(d, ring.size - d))
        self.slot, self.kib = links.slot(), kib(source(ring.pos))
        self.total = self.kib * len(order)
        for d in order:
            links.send(self.slot, source(ring.at(d)), target(ring.pos, d), ring.device(d))
        wide = ring.size > 4
        self.due = links.clock.sent(ring.axis, self.kib * (9 if wide else 3), 1.9 if wide else 2.6)

    def final(self):
        self.links.arrived(self.slot, self.total)


def summed_block(ring, own, landing, relay, direct):
    if not direct:
        halves = yield from ReduceScatter(ring, own, relay).flow()
        return halves
    whole = own(ring.pos, None)
    moved = Direct(ring, lambda o: own(o, None), lambda o, d: landing.at[d])
    yield moved.due
    moved.final()
    total = whole[...]
    for d in range(1, ring.size):
        total = total + landing[d]
    return [total[:8], total[8:]]


def gathered(ring, full, half, direct):
    if not direct:
        yield from AllGather(ring, full, half).flow()
    else:
        moved = Direct(ring, lambda o: full(ring.pos), lambda o, d: full(o))
        yield moved.due
        moved.final()


def rows8(h):
    return slice(None) if h is None else pl.ds(8 * h, 8)


def place():
    y, s, c = lax.axis_index("view"), lax.axis_index("sent"), lax.axis_index("col")
    return y, s // NZ, lax.rem(s, NZ), c


def rings(links, x, z, y):
    def x_dev(delta):
        return {"sent": lax.rem(x + (delta % NX), NX) * NZ + z}

    def z_dev(delta):
        return {"sent": x * NZ + lax.rem(z + (delta % NZ), NZ)}

    def y_dev(delta):
        return {"view": lax.rem(y + (delta % NY), NY)}

    return (Ring(links, "x", NX, x, x_dev), Ring(links, "z", NZ, z, z_dev), Ring(links, "y", NY, y, y_dev))


def nt(a, b):
    return lax.dot_general(a, b, (((1,), (1,)), ((), ())), precision=HIGH, preferred_element_type=F32)


def nn(a, b):
    return lax.dot_general(a, b, (((1,), (0,)), ((), ())), precision=HIGH, preferred_element_type=F32)


CHAINS = (
    (0, 0, 0.0, "z", "z", (True, True, True, True, True, False)),
    (0, 1, 0.03, "x", "z", (False, True, True, True, True, False)),
    (1, 0, 1.02, "x", "x", (False, True, True, True, True, True)),
    (1, 1, 1.05, "z", "x", (True, False, True, True, True, True)),
    (2, 0, 2.04, "z", "z", (True, True, True, True, True, False)),
    (2, 1, 10.01, "z", "x", (True, True, True, True, True, True)),
)
INV_START = 12.0


def project(scale, widths, shared, inv, sketched, loadings, merged_out, gram_out,
            feats, sharedH, sharedT, terms, land_x, land_xz, land_z, land_zx, quarter, slab, proj, invx, hop,
            part, part_in, part_sum, land_h, half, back, land_b, loadT, stage, merged, gram, land_8, land_4,
            contrib, mine_in, mine_sum, land_m, outer, outer_in, outer_sum, from_y, sum_y, over_x, over_z,
            send_sems, recv_sems, feat_sems, own_sems, out_sems):
    y, x, z, c = place()
    links = Links(send_sems, recv_sems, stage)
    clock = links.clock
    rx, rz, ry = rings(links, x, z, y)
    partner = {"col": 1 - c}

    bring_shared = pltpu.make_async_copy(shared, sharedH, own_sems.at[0])
    bring_shared.start()
    barrier = pltpu.get_barrier_semaphore()
    peers = [partner] + [ring.device(d) for ring in (rx, rz, ry) for d in range(1, ring.size)]
    for peer in peers:
        pl.semaphore_signal(barrier, inc=1, device_id=peer, device_id_type=MESH)

    def columns(q):
        return pl.ds(pl.multiple_of(q * 256, 256), 256)

    quarters = [rx.at(d) for d in (2, 3, 1, 0)]
    loads = {}
    for v in range(3):
        for n, q in enumerate(quarters):
            loads[v, n] = pltpu.make_async_copy(sketched.at[v, :, columns(q)], feats.at[v, q], feat_sems.at[4 * v + n])
            loads[v, n].start()
    own_inv = pltpu.make_async_copy(inv.at[:, :, columns(x)], invx.at[:, x], own_sems.at[1])
    own_inv.start()
    bring_shared.wait()
    sharedT[...] = sharedH[...].T

    first_col = c * 1024 + x * 256
    lane = lax.broadcasted_iota(jnp.int32, (8, 256), 1)
    row = (lane // 64) * (64 * NZ) + z * 64 + lax.rem(lane, 64)

    def lanes_kept(v, value):
        return jnp.where(first_col + lane < widths[v], value, 0.0)

    inv_slots = {(v, kind): links.slot() for v in range(3) for kind in ("near", "hop", "far")}

    def inv_flow():
        for v in range(3):
            for i, sign in enumerate((1, -1)):
                links.send(inv_slots[v, "near"], inv.at[v, :, columns(rx.at(sign))], invx.at[v, x], rx.device(sign))
                links.send(inv_slots[v, "hop"], inv.at[v, pl.ds(32 * i, 32), columns(rx.at(2))],
                           hop.at[v, i], rx.device(sign))
            due = clock.sent("x", 96)
            yield clock.now
        yield due
        for v in range(3):
            links.arrived(inv_slots[v, "hop"], 64)
            for i, sign in enumerate((1, -1)):
                links.send(inv_slots[v, "far"], hop.at[v, i], invx.at[v, rx.at(-sign), pl.ds(32 * i, 32)],
                           rx.device(sign))
            due = clock.sent("x", 32)
            yield clock.now

    sending_inv = inv_flow()
    inv_here = set()

    def need_inv(v):
        for _ in sending_inv:
            pass
        if not inv_here:
            own_inv.wait()
        if v not in inv_here:
            inv_here.add(v)
            links.arrived(inv_slots[v, "near"], 128)
            links.arrived(inv_slots[v, "far"], 64)

    def swap(src, dst):
        slot = links.slot()
        links.send(slot, src, dst, partner)
        yield clock.now + 1.55
        links.arrived(slot, kib(src))

    used = []

    def use(v, k, q):
        block = loadT[v, k, q].reshape(128, 256).T
        stage[v, columns(q), 128 * k:128 * k + 128] = block
        product = jnp.dot(feats[v, q], block.astype(BF16), preferred_element_type=F32).reshape(2, NY, 128, 128)
        contrib[k] = contrib[k] + product if k in used else product
        used.append(k)

    made = set()

    def make_terms(v):
        if v in made:
            return
        made.add(v)
        for n, q in enumerate(quarters):
            loads[v, n].wait()
            terms[v, :, q] = jnp.dot(sharedT[...], feats[v, q], preferred_element_type=F32).reshape(2, NZ, 16, 256)
        if len(made) == 1:
            pl.semaphore_wait(barrier, len(peers))

    def merge_flow(k):
        slots = {d: links.slot() for d in (2, 1, 3, 0)}
        for d, slot in slots.items():
            links.send(slot, contrib.at[k, 1 - c, ry.at(d)], mine_in.at[k, ry.at(d)], partner)
        yield clock.now + 1.55

        def summed(d):
            o = ry.at(d)
            links.arrived(slots[d], 64)
            mine_sum[k, o] = contrib[k, c, o] + mine_in[k, o]

        ms = ReduceScatter(ry, lambda o, h: mine_sum.at[k, o, pl.ds(64 * h, 64)], land_m.at[k])
        summed(2)
        due = ms.step(1, 0)
        summed(1)
        summed(3)
        ms.step(1, 1)
        summed(0)
        yield due
        yield ms.step(2, 0)
        halves = ms.final()
        for h in (0, 1):
            merged[c, y, pl.ds(64 * h, 64), 128 * k:128 * k + 128] = halves[h]

    finished = []

    def chain(v, k, first, last, direct):
        make_terms(v)
        if first == "x":
            halves = yield from ReduceScatter(
                rx, lambda o, h: terms.at[v, k, o, pl.ds(4 * h, 4)], land_x.at[v, k]).flow()
            for h in (0, 1):
                quarter[v, k, pl.ds(4 * h, 4)] = halves[h]
            halves = yield from summed_block(
                rz, lambda o, h: quarter.at[v, k, o, rows8(h)], land_8.at[v, k, 0], land_xz.at[v, k], direct[0])
        else:
            halves = yield from ReduceScatter(
                rz, lambda o, h: terms.at[v, k, :, o, pl.ds(8 * h, 8)], land_z.at[v, k]).flow()
            for h in (0, 1):
                slab[v, k, :, pl.ds(8 * h, 8)] = halves[h]
            halves = yield from summed_block(
                rx, lambda o, h: slab.at[v, k, o, rows8(h)], land_4.at[v, k, 0], land_zx.at[v, k], direct[0])
        for h in (0, 1):
            proj[v, k, z, pl.ds(8 * h, 8)] = lanes_kept(v, halves[h] * scale)
        yield from gathered(rz, lambda o: proj.at[v, k, o], lambda o, h: proj.at[v, k, o, rows8(h)], direct[1])

        need_inv(v)
        part[v, k] = nt(proj[v, k].reshape(128, 256), invx[v].reshape(256, 256)).reshape(2, NX, 16, 256)
        yield from swap(part.at[v, k, 1 - c], part_in.at[v, k])
        part_sum[v, k] = part[v, k, c] + part_in[v, k]
        halves = yield from summed_block(
            rx, lambda o, h: part_sum.at[v, k, o, rows8(h)], land_4.at[v, k, 1], land_h.at[v, k], direct[2])
        for h in (0, 1):
            half[v, k, c, x, pl.ds(8 * h, 8)] = jnp.where(row < widths[v], halves[h], 0.0)
        yield from gathered(rx, lambda o: half.at[v, k, c, o], lambda o, h: half.at[v, k, c, o, rows8(h)], direct[3])
        yield from swap(half.at[v, k, c], half.at[v, k, c])

        back[v, k] = nn(half[v, k].reshape(128, 256), invx[v].reshape(256, 256)).reshape(NZ, 16, 256)
        halves = yield from summed_block(
            rz, lambda o, h: back.at[v, k, o, rows8(h)], land_8.at[v, k, 1], land_b.at[v, k], direct[4])
        for h in (0, 1):
            loadT[v, k, x, z, pl.ds(8 * h, 8)] = lanes_kept(v, halves[h])
        if last == "x":
            yield from gathered(
                rx, lambda o: loadT.at[v, k, o, z], lambda o, h: loadT.at[v, k, o, z, rows8(h)], direct[5])
            yield from AllGather(
                rz, lambda o: loadT.at[v, k, :, o], lambda o, h: loadT.at[v, k, :, o, pl.ds(8 * h, 8)]).flow()
            for q in range(NX):
                use(v, k, q)
        else:
            yield from gathered(
                rz, lambda o: loadT.at[v, k, x, o], lambda o, h: loadT.at[v, k, x, o, rows8(h)], direct[5])

            def reached(t):
                for d in sorted({t % NX, -t % NX}):
                    use(v, k, rx.at(d))

            yield from AllGather(
                rx, lambda o: loadT.at[v, k, o], lambda o, h: loadT.at[v, k, o, pl.ds(4 * h, 4)]).flow(reached)
        finished.append(k)
        if finished.count(k) == 3:
            yield from merge_flow(k)

    for v, k, start, first, last, direct in CHAINS:
        clock.add(start, chain(v, k, first, last, direct))
    clock.add(INV_START, sending_inv)
    clock.run()
    put_loadings = pltpu.make_async_copy(stage, loadings, out_sems.at[0])
    put_loadings.start()

    rows = merged[c, y]

    outer[...] = tn(rows, rows).reshape(2, NY, 32, 256)
    slot = links.slot()
    links.send(slot, outer.at[1 - c], outer_in, partner)
    links.arrived(slot, 128)
    outer_sum[...] = outer[c] + outer_in[...]
    gs = Direct(ry, lambda o: outer_sum.at[o], lambda o, d: from_y.at[o])
    mg = AllGather(ry, lambda o: merged.at[c, o], lambda o, h: merged.at[c, o, pl.ds(64 * h, 64)])
    from_y[y] = outer_sum[y]
    gs.final()
    mg.step(1)
    sum_y[...] = ((from_y[0] + from_y[1]) + (from_y[2] + from_y[3])).reshape(NX, 8, 256)
    over_x[x] = sum_y[x]
    Direct(rx, lambda o: sum_y.at[o], lambda o, d: over_x.at[o]).final()
    over_z[z] = (over_x[0] + over_x[1]) + (over_x[2] + over_x[3])
    gz = Direct(rz, lambda o: over_z.at[z], lambda o, d: over_z.at[o])
    mg.step(2)
    gz.final()
    acc = over_z[0]
    for i in range(1, NZ):
        acc = acc + over_z[i]
    gram[c, y, x] = acc
    gx = Direct(rx, lambda o: gram.at[c, y, x], lambda o, d: gram.at[c, y, o])
    mg.final()
    slot = links.slot()
    links.send(slot, merged.at[c], merged.at[c], partner)
    gx.final()
    gy = Direct(ry, lambda o: gram.at[c, y], lambda o, d: gram.at[c, o])
    links.arrived(slot, 512)
    put_merged = pltpu.make_async_copy(merged, merged_out, out_sems.at[1])
    put_merged.start()
    gy.final()
    last = links.slot()
    links.send(last, gram.at[c], gram.at[c], partner)
    links.arrived(last, 128)
    put_gram = pltpu.make_async_copy(gram, gram_out, out_sems.at[2])
    put_gram.start()
    put_loadings.wait()
    put_merged.wait()
    links.drain()
    put_gram.wait()


PANEL = 32


def panel_inverse(tiles, lane0):
    groups = PANEL // 8
    sub = lax.broadcasted_iota(jnp.int32, (8, 128), 0)
    lane = lax.broadcasted_iota(jnp.int32, (8, 128), 1)

    def spread(tile, s):
        return jnp.broadcast_to(tile[s:s + 1, :], (8, 128))

    cols = [{g: jnp.broadcast_to(tiles[g][:, lane0 + j:lane0 + j + 1], (8, 128)) for g in range(j // 8, groups)}
            for j in range(PANEL)]
    unit = [jnp.where(lane == sub + 8 * g, 1.0, 0.0).astype(F32) for g in range(groups)]
    pivots = [jnp.ones((8, 128), F32) for g in range(groups)]
    for k in range(PANEL):
        gk, sk = divmod(k, 8)
        pivot = spread(cols[k][gk], sk)
        inverse = 1.0 / pivot
        pivots[gk] = jnp.where(sub == sk, pivot, pivots[gk])
        mult = {g: cols[k][g] * inverse for g in range(gk, groups)}
        for j in range(k + 1, PANEL):
            gj, sj = divmod(j, 8)
            entry = spread(cols[k][gj], sj)
            for g in range(gj, groups):
                cols[j][g] = cols[j][g] - mult[g] * entry
        row = spread(unit[gk], sk)
        for g in range(gk, groups):
            m = jnp.where(sub > sk, mult[g], 0.0) if g == gk else mult[g]
            unit[g] = unit[g] - m * row
    return jnp.concatenate([unit[g] * lax.rsqrt(pivots[g]) for g in range(groups)], axis=0)[:, :PANEL]


def tn(a, b):
    return lax.dot_general(a, b, (((0,), (0,)), ((), ())), precision=HIGH, preferred_element_type=F32)


def factor_inverse(work, inverse, between):
    n = work.shape[0]
    for p in range(n // PANEL):
        r0 = p * PANEL
        lt = r0 // 128 * 128
        tiles = [work[r0 + 8 * g:r0 + 8 * g + 8, lt:lt + 128] for g in range(PANEL // 8)]
        block = panel_inverse(tiles, r0 - lt)
        col = lax.broadcasted_iota(jnp.int32, (PANEL, n), 1)
        row = lax.broadcasted_iota(jnp.int32, (PANEL, n), 0)
        here = (col >= r0) & (col < r0 + PANEL)
        wide = jnp.where(here, jnp.where(col == row + r0, 1.0, 0.0), work[r0:r0 + PANEL, :])
        u = nn(block, wide)
        inverse[r0:r0 + PANEL, :] = jnp.where(col < r0 + PANEL, u, 0.0)
        between(p)
        r1 = r0 + PANEL
        if r1 < n:
            base = r1 // 128 * 128
            upd = tn(u[:, base:], u)[r1 - base:]
            col = lax.broadcasted_iota(jnp.int32, (n - r1, n), 1)
            here = (col >= r0) & (col < r1)
            work[r1:, :] = jnp.where(here, 0.0, work[r1:, :]) - upd


def solve(root, gram, merged, loaded, updated, loadings, work, inverse, rows, passing, solved, sems):
    bring_gram = pltpu.make_async_copy(gram, work, sems.at[0])
    bring_rows = pltpu.make_async_copy(merged, rows, sems.at[1])
    bring = pltpu.make_async_copy(loaded, passing, sems.at[2])
    put = pltpu.make_async_copy(passing, loadings, sems.at[3])
    bring_gram.start()
    bring_rows.start()
    bring.start()
    bring_gram.wait()

    def between(panel):
        if panel == 2:
            bring.wait()
            put.start()

    factor_inverse(work, inverse, between)
    bring_rows.wait()
    puts = []
    for i in range(4):
        here = slice(256 * i, 256 * i + 256)
        solved[here, :] = nt(rows[here, :], inverse[...]) * root
        puts.append(pltpu.make_async_copy(solved.at[here], updated.at[here], sems.at[4 + i]))
        puts[-1].start()
    put.wait()
    for copy in puts:
        copy.wait()


def shards(sketched, widths, inv_factor, shared):
    total_rows = shared.shape[0] * lax.axis_size("sent")
    smem, hbm = (pl.BlockSpec(memory_space=m) for m in (pltpu.SMEM, pltpu.HBM))

    def buf(*shape):
        return pltpu.VMEM(shape, F32)

    sems = [pltpu.SemaphoreType.DMA((SEND_SEMS,)), pltpu.SemaphoreType.DMA((RECV_SEMS,))]

    def kernel_a(*refs):
        project(1.0 / math.sqrt(total_rows), *refs)

    loadings, merged, gram = pl.pallas_call(
        kernel_a,
        name="project",
        out_shape=(jax.ShapeDtypeStruct((3, 1024, 256), F32), jax.ShapeDtypeStruct((2, NY, 128, 256), F32),
                   jax.ShapeDtypeStruct((2, NY, NX, 8, 256), F32)),
        in_specs=[smem, hbm, hbm, hbm],
        out_specs=(hbm, hbm, hbm),
        scratch_shapes=[
            pltpu.VMEM((3, 4, 1024, 256), BF16), pltpu.VMEM((1024, 256), BF16), pltpu.VMEM((256, 1024), BF16),
            buf(3, 2, 4, 8, 16, 256), buf(3, 2, 2, 2, 2, 4, 16, 256), buf(3, 2, 2, 2, 4, 8, 256),
            buf(3, 2, 2, 2, 4, 4, 8, 256), buf(3, 2, 2, 2, 2, 8, 256), buf(3, 2, 8, 16, 256), buf(3, 2, 4, 16, 256),
            buf(3, 2, 8, 16, 256), buf(3, 4, 64, 256), buf(3, 2, 32, 256),
            buf(3, 2, 2, 4, 16, 256), buf(3, 2, 4, 16, 256), buf(3, 2, 4, 16, 256), buf(3, 2, 2, 2, 2, 8, 256),
            buf(3, 2, 2, 4, 16, 256), buf(3, 2, 8, 16, 256), buf(3, 2, 2, 2, 4, 8, 256), buf(3, 2, 4, 8, 16, 256),
            buf(3, 1024, 256), buf(2, NY, 128, 256), buf(2, NY, NX, 8, 256), buf(3, 2, 2, 8, 16, 256), buf(3, 2, 2, 4, 16, 256),
            buf(2, 2, 4, 128, 128), buf(2, 4, 128, 128), buf(2, 4, 128, 128), buf(2, 2, 2, 2, 64, 128), buf(2, 4, 32, 256),
            buf(4, 32, 256), buf(4, 32, 256), buf(4, 32, 256), buf(4, 8, 256), buf(4, 8, 256), buf(8, 8, 256), *sems,
            pltpu.SemaphoreType.DMA((12,)), pltpu.SemaphoreType.DMA((2,)), pltpu.SemaphoreType.DMA((3,))],
        compiler_params=pltpu.CompilerParams(collective_id=0, has_side_effects=True, vmem_limit_bytes=58 * 2**20),
    )(widths, shared, inv_factor, sketched)
    merged, gram = merged.reshape(1024, 256), gram.reshape(256, 256)

    def kernel_c(*refs):
        solve(math.sqrt(total_rows), *refs)

    updated, loadings = pl.pallas_call(
        kernel_c,
        name="solve",
        out_shape=(jax.ShapeDtypeStruct((1024, 256), F32), jax.ShapeDtypeStruct((3, 1024, 256), F32)),
        in_specs=[hbm, hbm, hbm],
        out_specs=(hbm, hbm),
        scratch_shapes=[buf(256, 256), buf(256, 256), buf(1024, 256), buf(3, 1024, 256), buf(1024, 256),
                        pltpu.SemaphoreType.DMA((8,))],
        compiler_params=pltpu.CompilerParams(vmem_limit_bytes=58 * 2**20),
    )(gram, merged, loadings)
    return (loadings, updated)


def solution(mesh):
    return jax.shard_map(
        shards,
        mesh=mesh,
        in_specs=(P("view", "sent", "col"), P("view"), P("view", "sent", "col"), P("sent", None)),
        out_specs=(P("view", "col", None), P("sent", None)),
        check_vma=False,
    )
```

```python
import math

import jax
import jax.numpy as jnp
from jax import lax
from jax.experimental import pallas as pl
from jax.experimental.pallas import tpu as pltpu
from jax.sharding import PartitionSpec as P

MESH = pl.DeviceIdType.MESH
HIGH = lax.Precision.HIGHEST
F32 = jnp.float32
BF16 = jnp.bfloat16
NX, NZ, NY = 4, 8, 4
SEND_SEMS, RECV_SEMS = 12, 157


class Clock:
    def __init__(self):
        self.now, self.busy, self.flows = 0.0, {}, []

    def sent(self, axis, kib, latency=3.5):
        self.busy[axis] = max(self.now, self.busy.get(axis, 0.0)) + kib * 0.0225
        return self.busy[axis] + latency

    def add(self, start, flow):
        self.flows.append([start, len(self.flows), flow])

    def run(self):
        while self.flows:
            item = min(self.flows)
            self.now = max(self.now, item[0]) + 0.1
            try:
                item[0] = next(item[2])
            except StopIteration:
                self.flows.remove(item)


def kib(ref):
    return math.prod(ref.shape) * 4 // 1024


class Links:
    def __init__(self, send_sems, recv_sems, ruler):
        self.send_sems, self.recv_sems, self.ruler = send_sems, recv_sems, ruler
        self.used, self.groups, self.clock = 0, [], Clock()

    def slot(self):
        self.used += 1
        assert self.used <= RECV_SEMS
        return self.used - 1

    def send(self, slot, src, dst, device):
        size = kib(src)
        if not self.groups or self.groups[-1] + size > 1024:
            self.groups.append(0)
            assert len(self.groups) <= SEND_SEMS
        self.groups[-1] += size
        pltpu.make_async_remote_copy(
            src_ref=src, dst_ref=dst, send_sem=self.send_sems.at[len(self.groups) - 1],
            recv_sem=self.recv_sems.at[slot], device_id=device, device_id_type=MESH).start()

    def wait(self, sem, size):
        rows = self.ruler.at[0, pl.ds(0, size)]
        pltpu.make_async_copy(rows, rows, sem).wait()

    def arrived(self, slot, size):
        self.wait(self.recv_sems.at[slot], size)

    def drain(self):
        for group, size in enumerate(self.groups):
            self.wait(self.send_sems.at[group], size)


class Ring:
    def __init__(self, links, axis, size, pos, device):
        self.links, self.axis, self.size, self.pos, self.device = links, axis, size, pos, device

    def at(self, delta):
        return lax.rem(self.pos + (delta % self.size), self.size)


class ReduceScatter:
    def __init__(self, ring, own, landing):
        self.ring, self.own, self.landing = ring, own, landing
        self.kib = kib(landing.at[0, 0, 0])
        self.half_ring = ring.size // 2
        self.slots = {(kind, t): ring.links.slot()
                      for t in range(1, self.half_ring + 1) for kind in (0, 1)
                      if not (kind == 1 and t == self.half_ring)}

    def wait(self, kind, t):
        self.ring.links.arrived(self.slots[kind, t], 2 * self.kib)

    def step(self, t, kind):
        if t > 1:
            self.wait(kind, t - 1)
        for d, sign in ((0, -1), (1, 1)):
            dist = self.half_ring + 1 - t - kind
            src = self.own(self.ring.at(sign * dist), d if kind == 0 else 1 - d)
            if t > 1:
                buf = self.landing.at[d, kind, t - 2]
                buf[...] = buf[...] + src[...]
                src = buf
            self.ring.links.send(self.slots[kind, t], src, self.landing.at[d, kind, t - 1], self.ring.device(sign))
        return self.ring.links.clock.sent(self.ring.axis, self.kib)

    def flow(self):
        due = {}
        for t in range(1, self.half_ring + 1):
            for kind in (0, 1):
                if (kind, t) not in self.slots:
                    continue
                if t > 1:
                    yield due[kind]
                due[kind] = self.step(t, kind)
        yield max(due.values())
        return self.final()

    def final(self):
        last = self.half_ring
        self.wait(0, last)
        self.wait(1, last - 1)
        return [self.own(self.ring.pos, h)[...] + self.landing[h, 0, last - 1] + self.landing[1 - h, 1, last - 2]
                for h in (0, 1)]


class AllGather:
    def __init__(self, ring, full, half):
        self.ring, self.full, self.half = ring, full, half
        self.kib = kib(full(ring.pos))
        self.half_ring = ring.size // 2
        self.slots = {t: ring.links.slot() for t in range(1, self.half_ring + 1)}

    def wait(self, t):
        self.ring.links.arrived(self.slots[t], 2 * self.kib if t < self.half_ring else self.kib)

    def step(self, t):
        if t > 1:
            self.wait(t - 1)
        for d, sign in ((0, -1), (1, 1)):
            owner = self.ring.at(-sign * (t - 1))
            src = self.half(owner, d) if t == self.half_ring else self.full(owner)
            self.ring.links.send(self.slots[t], src, src, self.ring.device(sign))
        return self.ring.links.clock.sent(self.ring.axis, self.kib if t < self.half_ring else self.kib / 2)

    def final(self):
        self.wait(self.half_ring)

    def flow(self, reached=None):
        for t in range(1, self.half_ring + 1):
            due = self.step(t)
            if reached is not None:
                reached(t - 1)
            yield due
        self.final()
        if reached is not None:
            reached(self.half_ring)


class Direct:
    def __init__(self, ring, source, target):
        links = self.links = ring.links
        order = sorted(range(1, ring.size), key=lambda d: -min(d, ring.size - d))
        self.slot, self.kib = links.slot(), kib(source(ring.pos))
        self.total = self.kib * len(order)
        for d in order:
            links.send(self.slot, source(ring.at(d)), target(ring.pos, d), ring.device(d))
        wide = ring.size > 4
        self.due = links.clock.sent(ring.axis, self.kib * (9 if wide else 3), 1.9 if wide else 2.6)

    def final(self):
        self.links.arrived(self.slot, self.total)


def summed_block(ring, own, landing, relay, direct):
    if not direct:
        halves = yield from ReduceScatter(ring, own, relay).flow()
        return halves
    whole = own(ring.pos, None)
    moved = Direct(ring, lambda o: own(o, None), lambda o, d: landing.at[d])
    yield moved.due
    moved.final()
    total = whole[...]
    for d in range(1, ring.size):
        total = total + landing[d]
    return [total[:8], total[8:]]


def gathered(ring, full, half, direct):
    if not direct:
        yield from AllGather(ring, full, half).flow()
    else:
        moved = Direct(ring, lambda o: full(ring.pos), lambda o, d: full(o))
        yield moved.due
        moved.final()


def rows8(h):
    return slice(None) if h is None else pl.ds(8 * h, 8)


def place():
    y, s, c = lax.axis_index("view"), lax.axis_index("sent"), lax.axis_index("col")
    return y, s // NZ, lax.rem(s, NZ), c


def rings(links, x, z, y):
    def x_dev(delta):
        return {"sent": lax.rem(x + (delta % NX), NX) * NZ + z}

    def z_dev(delta):
        return {"sent": x * NZ + lax.rem(z + (delta % NZ), NZ)}

    def y_dev(delta):
        return {"view": lax.rem(y + (delta % NY), NY)}

    return (Ring(links, "x", NX, x, x_dev), Ring(links, "z", NZ, z, z_dev), Ring(links, "y", NY, y, y_dev))


def nt(a, b):
    return lax.dot_general(a, b, (((1,), (1,)), ((), ())), precision=HIGH, preferred_element_type=F32)


def nn(a, b):
    return lax.dot_general(a, b, (((1,), (0,)), ((), ())), precision=HIGH, preferred_element_type=F32)


CHAINS = (
    (0, 0, 0.0, "z", "z", (True, True, True, True, True, False)),
    (0, 1, 0.03, "x", "z", (False, True, True, True, True, False)),
    (1, 0, 1.02, "x", "x", (False, True, True, True, True, True)),
    (1, 1, 1.05, "z", "x", (True, False, True, True, True, True)),
    (2, 0, 2.04, "z", "z", (True, True, True, True, True, False)),
    (2, 1, 10.01, "z", "x", (True, True, True, True, True, True)),
)
INV_START = 12.0


def project(scale, widths, shared, inv, sketched, loadings, merged_out, gram_out,
            feats, sharedH, sharedT, terms, land_x, land_xz, land_z, land_zx, quarter, slab, proj, invx, hop,
            part, part_in, part_sum, land_h, half, back, land_b, loadT, stage, merged, gram, land_8, land_4,
            contrib, mine_in, mine_sum, land_m, outer, outer_in, outer_sum, from_y, sum_y, over_x, over_z,
            send_sems, recv_sems, feat_sems, own_sems, out_sems):
    y, x, z, c = place()
    links = Links(send_sems, recv_sems, stage)
    clock = links.clock
    rx, rz, ry = rings(links, x, z, y)
    partner = {"col": 1 - c}

    bring_shared = pltpu.make_async_copy(shared, sharedH, own_sems.at[0])
    bring_shared.start()
    barrier = pltpu.get_barrier_semaphore()
    peers = [partner] + [ring.device(d) for ring in (rx, rz, ry) for d in range(1, ring.size)]
    for peer in peers:
        pl.semaphore_signal(barrier, inc=1, device_id=peer, device_id_type=MESH)

    def columns(q):
        return pl.ds(pl.multiple_of(q * 256, 256), 256)

    quarters = [rx.at(d) for d in (2, 3, 1, 0)]
    loads = {}
    for v in range(3):
        for n, q in enumerate(quarters):
            loads[v, n] = pltpu.make_async_copy(sketched.at[v, :, columns(q)], feats.at[v, q], feat_sems.at[4 * v + n])
            loads[v, n].start()
    own_inv = pltpu.make_async_copy(inv.at[:, :, columns(x)], invx.at[:, x], own_sems.at[1])
    own_inv.start()
    bring_shared.wait()
    sharedT[...] = sharedH[...].T

    first_col = c * 1024 + x * 256
    lane = lax.broadcasted_iota(jnp.int32, (8, 256), 1)
    row = (lane // 64) * (64 * NZ) + z * 64 + lax.rem(lane, 64)

    def lanes_kept(v, value):
        return jnp.where(first_col + lane < widths[v], value, 0.0)

    inv_slots = {(v, kind): links.slot() for v in range(3) for kind in ("near", "hop", "far")}

    def inv_flow():
        for v in range(3):
            for i, sign in enumerate((1, -1)):
                links.send(inv_slots[v, "near"], inv.at[v, :, columns(rx.at(sign))], invx.at[v, x], rx.device(sign))
                links.send(inv_slots[v, "hop"], inv.at[v, pl.ds(32 * i, 32), columns(rx.at(2))],
                           hop.at[v, i], rx.device(sign))
            due = clock.sent("x", 96)
            yield clock.now
        yield due
        for v in range(3):
            links.arrived(inv_slots[v, "hop"], 64)
            for i, sign in enumerate((1, -1)):
                links.send(inv_slots[v, "far"], hop.at[v, i], invx.at[v, rx.at(-sign), pl.ds(32 * i, 32)],
                           rx.device(sign))
            due = clock.sent("x", 32)
            yield clock.now

    sending_inv = inv_flow()
    inv_here = set()

    def need_inv(v):
        for _ in sending_inv:
            pass
        if not inv_here:
            own_inv.wait()
        if v not in inv_here:
            inv_here.add(v)
            links.arrived(inv_slots[v, "near"], 128)
            links.arrived(inv_slots[v, "far"], 64)

    def swap(src, dst):
        slot = links.slot()
        links.send(slot, src, dst, partner)
        yield clock.now + 1.55
        links.arrived(slot, kib(src))

    used = []

    def use(v, k, q):
        block = loadT[v, k, q].reshape(128, 256).T
        stage[v, columns(q), 128 * k:128 * k + 128] = block
        product = jnp.dot(feats[v, q], block.astype(BF16), preferred_element_type=F32).reshape(2, NY, 128, 128)
        contrib[k] = contrib[k] + product if k in used else product
        used.append(k)

    made = set()

    def make_terms(v):
        if v in made:
            return
        made.add(v)
        for n, q in enumerate(quarters):
            loads[v, n].wait()
            terms[v, :, q] = jnp.dot(sharedT[...], feats[v, q], preferred_element_type=F32).reshape(2, NZ, 16, 256)
        if len(made) == 1:
            pl.semaphore_wait(barrier, len(peers))

    def merge_flow(k):
        slots = {d: links.slot() for d in (2, 1, 3, 0)}
        for d, slot in slots.items():
            links.send(slot, contrib.at[k, 1 - c, ry.at(d)], mine_in.at[k, ry.at(d)], partner)
        yield clock.now + 1.55

        def summed(d):
            o = ry.at(d)
            links.arrived(slots[d], 64)
            mine_sum[k, o] = contrib[k, c, o] + mine_in[k, o]

        ms = ReduceScatter(ry, lambda o, h: mine_sum.at[k, o, pl.ds(64 * h, 64)], land_m.at[k])
        summed(2)
        due = ms.step(1, 0)
        summed(1)
        summed(3)
        ms.step(1, 1)
        summed(0)
        yield due
        yield ms.step(2, 0)
        halves = ms.final()
        for h in (0, 1):
            merged[c, y, pl.ds(64 * h, 64), 128 * k:128 * k + 128] = halves[h]

    finished = []

    def chain(v, k, first, last, direct):
        make_terms(v)
        if first == "x":
            halves = yield from ReduceScatter(
                rx, lambda o, h: terms.at[v, k, o, pl.ds(4 * h, 4)], land_x.at[v, k]).flow()
            for h in (0, 1):
                quarter[v, k, pl.ds(4 * h, 4)] = halves[h]
            halves = yield from summed_block(
                rz, lambda o, h: quarter.at[v, k, o, rows8(h)], land_8.at[v, k, 0], land_xz.at[v, k], direct[0])
        else:
            halves = yield from ReduceScatter(
                rz, lambda o, h: terms.at[v, k, :, o, pl.ds(8 * h, 8)], land_z.at[v, k]).flow()
            for h in (0, 1):
                slab[v, k, :, pl.ds(8 * h, 8)] = halves[h]
            halves = yield from summed_block(
                rx, lambda o, h: slab.at[v, k, o, rows8(h)], land_4.at[v, k, 0], land_zx.at[v, k], direct[0])
        for h in (0, 1):
            proj[v, k, z, pl.ds(8 * h, 8)] = lanes_kept(v, halves[h] * scale)
        yield from gathered(rz, lambda o: proj.at[v, k, o], lambda o, h: proj.at[v, k, o, rows8(h)], direct[1])

        need_inv(v)
        part[v, k] = nt(proj[v, k].reshape(128, 256), invx[v].reshape(256, 256)).reshape(2, NX, 16, 256)
        yield from swap(part.at[v, k, 1 - c], part_in.at[v, k])
        part_sum[v, k] = part[v, k, c] + part_in[v, k]
        halves = yield from summed_block(
            rx, lambda o, h: part_sum.at[v, k, o, rows8(h)], land_4.at[v, k, 1], land_h.at[v, k], direct[2])
        for h in (0, 1):
            half[v, k, c, x, pl.ds(8 * h, 8)] = jnp.where(row < widths[v], halves[h], 0.0)
        yield from gathered(rx, lambda o: half.at[v, k, c, o], lambda o, h: half.at[v, k, c, o, rows8(h)], direct[3])
        yield from swap(half.at[v, k, c], half.at[v, k, c])

        back[v, k] = nn(half[v, k].reshape(128, 256), invx[v].reshape(256, 256)).reshape(NZ, 16, 256)
        halves = yield from summed_block(
            rz, lambda o, h: back.at[v, k, o, rows8(h)], land_8.at[v, k, 1], land_b.at[v, k], direct[4])
        for h in (0, 1):
            loadT[v, k, x, z, pl.ds(8 * h, 8)] = lanes_kept(v, halves[h])
        if last == "x":
            yield from gathered(
                rx, lambda o: loadT.at[v, k, o, z], lambda o, h: loadT.at[v, k, o, z, rows8(h)], direct[5])
            yield from AllGather(
                rz, lambda o: loadT.at[v, k, :, o], lambda o, h: loadT.at[v, k, :, o, pl.ds(8 * h, 8)]).flow()
            for q in range(NX):
                use(v, k, q)
        else:
            yield from gathered(
                rz, lambda o: loadT.at[v, k, x, o], lambda o, h: loadT.at[v, k, x, o, rows8(h)], direct[5])

            def reached(t):
                for d in sorted({t % NX, -t % NX}):
                    use(v, k, rx.at(d))

            yield from AllGather(
                rx, lambda o: loadT.at[v, k, o], lambda o, h: loadT.at[v, k, o, pl.ds(4 * h, 4)]).flow(reached)
        finished.append(k)
        if finished.count(k) == 3:
            yield from merge_flow(k)

    for v, k, start, first, last, direct in CHAINS:
        clock.add(start, chain(v, k, first, last, direct))
    clock.add(INV_START, sending_inv)
    clock.run()
    put_loadings = pltpu.make_async_copy(stage, loadings, out_sems.at[0])
    put_loadings.start()

    rows = merged[c, y]

    outer[...] = tn(rows, rows).reshape(2, NY, 32, 256)
    slot = links.slot()
    links.send(slot, outer.at[1 - c], outer_in, partner)
    links.arrived(slot, 128)
    outer_sum[...] = outer[c] + outer_in[...]
    gs = Direct(ry, lambda o: outer_sum.at[o], lambda o, d: from_y.at[o])
    mg = AllGather(ry, lambda o: merged.at[c, o], lambda o, h: merged.at[c, o, pl.ds(64 * h, 64)])
    from_y[y] = outer_sum[y]
    gs.final()
    mg.step(1)
    sum_y[...] = ((from_y[0] + from_y[1]) + (from_y[2] + from_y[3])).reshape(NX, 8, 256)
    over_x[x] = sum_y[x]
    Direct(rx, lambda o: sum_y.at[o], lambda o, d: over_x.at[o]).final()
    over_z[z] = (over_x[0] + over_x[1]) + (over_x[2] + over_x[3])
    gz = Direct(rz, lambda o: over_z.at[z], lambda o, d: over_z.at[o])
    mg.step(2)
    gz.final()
    acc = over_z[0]
    for i in range(1, NZ):
        acc = acc + over_z[i]
    gram[c, y, x] = acc
    gx = Direct(rx, lambda o: gram.at[c, y, x], lambda o, d: gram.at[c, y, o])
    mg.final()
    slot = links.slot()
    links.send(slot, merged.at[c], merged.at[c], partner)
    gx.final()
    gy = Direct(ry, lambda o: gram.at[c, y], lambda o, d: gram.at[c, o])
    links.arrived(slot, 512)
    put_merged = pltpu.make_async_copy(merged, merged_out, out_sems.at[1])
    put_merged.start()
    gy.final()
    last = links.slot()
    links.send(last, gram.at[c], gram.at[c], partner)
    links.arrived(last, 128)
    put_gram = pltpu.make_async_copy(gram, gram_out, out_sems.at[2])
    put_gram.start()
    put_loadings.wait()
    put_merged.wait()
    links.drain()
    put_gram.wait()


PANEL = 32


def panel_inverse(tiles, lane0):
    groups = PANEL // 8
    sub = lax.broadcasted_iota(jnp.int32, (8, 128), 0)
    lane = lax.broadcasted_iota(jnp.int32, (8, 128), 1)

    def spread(tile, s):
        return jnp.broadcast_to(tile[s:s + 1, :], (8, 128))

    cols = [{g: jnp.broadcast_to(tiles[g][:, lane0 + j:lane0 + j + 1], (8, 128)) for g in range(j // 8, groups)}
            for j in range(PANEL)]
    unit = [jnp.where(lane == sub + 8 * g, 1.0, 0.0).astype(F32) for g in range(groups)]
    pivots = [jnp.ones((8, 128), F32) for g in range(groups)]
    for k in range(PANEL):
        gk, sk = divmod(k, 8)
        pivot = spread(cols[k][gk], sk)
        inverse = 1.0 / pivot
        pivots[gk] = jnp.where(sub == sk, pivot, pivots[gk])
        mult = {g: cols[k][g] * inverse for g in range(gk, groups)}
        for j in range(k + 1, PANEL):
            gj, sj = divmod(j, 8)
            entry = spread(cols[k][gj], sj)
            for g in range(gj, groups):
                cols[j][g] = cols[j][g] - mult[g] * entry
        row = spread(unit[gk], sk)
        for g in range(gk, groups):
            m = jnp.where(sub > sk, mult[g], 0.0) if g == gk else mult[g]
            unit[g] = unit[g] - m * row
    return jnp.concatenate([unit[g] * lax.rsqrt(pivots[g]) for g in range(groups)], axis=0)[:, :PANEL]


def tn(a, b):
    return lax.dot_general(a, b, (((0,), (0,)), ((), ())), precision=HIGH, preferred_element_type=F32)


def factor_inverse(work, inverse, between):
    n = work.shape[0]
    for p in range(n // PANEL):
        r0 = p * PANEL
        lt = r0 // 128 * 128
        tiles = [work[r0 + 8 * g:r0 + 8 * g + 8, lt:lt + 128] for g in range(PANEL // 8)]
        block = panel_inverse(tiles, r0 - lt)
        col = lax.broadcasted_iota(jnp.int32, (PANEL, n), 1)
        row = lax.broadcasted_iota(jnp.int32, (PANEL, n), 0)
        here = (col >= r0) & (col < r0 + PANEL)
        wide = jnp.where(here, jnp.where(col == row + r0, 1.0, 0.0), work[r0:r0 + PANEL, :])
        u = nn(block, wide)
        inverse[r0:r0 + PANEL, :] = jnp.where(col < r0 + PANEL, u, 0.0)
        between(p)
        r1 = r0 + PANEL
        if r1 < n:
            base = r1 // 128 * 128
            upd = tn(u[:, base:], u)[r1 - base:]
            col = lax.broadcasted_iota(jnp.int32, (n - r1, n), 1)
            here = (col >= r0) & (col < r1)
            work[r1:, :] = jnp.where(here, 0.0, work[r1:, :]) - upd


def solve(root, gram, merged, loaded, updated, loadings, work, inverse, rows, passing, solved, sems):
    bring_gram = pltpu.make_async_copy(gram, work, sems.at[0])
    bring_rows = pltpu.make_async_copy(merged, rows, sems.at[1])
    bring = pltpu.make_async_copy(loaded, passing, sems.at[2])
    put = pltpu.make_async_copy(passing, loadings, sems.at[3])
    bring_gram.start()
    bring_rows.start()
    bring.start()
    bring_gram.wait()

    def between(panel):
        if panel == 2:
            bring.wait()
            put.start()

    factor_inverse(work, inverse, between)
    bring_rows.wait()
    puts = []
    for i in range(4):
        here = slice(256 * i, 256 * i + 256)
        solved[here, :] = nt(rows[here, :], inverse[...]) * root
        puts.append(pltpu.make_async_copy(solved.at[here], updated.at[here], sems.at[4 + i]))
        puts[-1].start()
    put.wait()
    for copy in puts:
        copy.wait()


def shards(sketched, widths, inv_factor, shared):
    total_rows = shared.shape[0] * lax.axis_size("sent")
    smem, hbm = (pl.BlockSpec(memory_space=m) for m in (pltpu.SMEM, pltpu.HBM))

    def buf(*shape):
        return pltpu.VMEM(shape, F32)

    sems = [pltpu.SemaphoreType.DMA((SEND_SEMS,)), pltpu.SemaphoreType.DMA((RECV_SEMS,))]

    def kernel_a(*refs):
        project(1.0 / math.sqrt(total_rows), *refs)

    loadings, merged, gram = pl.pallas_call(
        kernel_a,
        name="project",
        out_shape=(jax.ShapeDtypeStruct((3, 1024, 256), F32), jax.ShapeDtypeStruct((2, NY, 128, 256), F32),
                   jax.ShapeDtypeStruct((2, NY, NX, 8, 256), F32)),
        in_specs=[smem, hbm, hbm, hbm],
        out_specs=(hbm, hbm, hbm),
        scratch_shapes=[
            pltpu.VMEM((3, 4, 1024, 256), BF16), pltpu.VMEM((1024, 256), BF16), pltpu.VMEM((256, 1024), BF16),
            buf(3, 2, 4, 8, 16, 256), buf(3, 2, 2, 2, 2, 4, 16, 256), buf(3, 2, 2, 2, 4, 8, 256),
            buf(3, 2, 2, 2, 4, 4, 8, 256), buf(3, 2, 2, 2, 2, 8, 256), buf(3, 2, 8, 16, 256), buf(3, 2, 4, 16, 256),
            buf(3, 2, 8, 16, 256), buf(3, 4, 64, 256), buf(3, 2, 32, 256),
            buf(3, 2, 2, 4, 16, 256), buf(3, 2, 4, 16, 256), buf(3, 2, 4, 16, 256), buf(3, 2, 2, 2, 2, 8, 256),
            buf(3, 2, 2, 4, 16, 256), buf(3, 2, 8, 16, 256), buf(3, 2, 2, 2, 4, 8, 256), buf(3, 2, 4, 8, 16, 256),
            buf(3, 1024, 256), buf(2, NY, 128, 256), buf(2, NY, NX, 8, 256), buf(3, 2, 2, 8, 16, 256), buf(3, 2, 2, 4, 16, 256),
            buf(2, 2, 4, 128, 128), buf(2, 4, 128, 128), buf(2, 4, 128, 128), buf(2, 2, 2, 2, 64, 128), buf(2, 4, 32, 256),
            buf(4, 32, 256), buf(4, 32, 256), buf(4, 32, 256), buf(4, 8, 256), buf(4, 8, 256), buf(8, 8, 256), *sems,
            pltpu.SemaphoreType.DMA((12,)), pltpu.SemaphoreType.DMA((2,)), pltpu.SemaphoreType.DMA((3,))],
        compiler_params=pltpu.CompilerParams(collective_id=0, has_side_effects=True, vmem_limit_bytes=58 * 2**20),
    )(widths, shared, inv_factor, sketched)
    merged, gram = merged.reshape(1024, 256), gram.reshape(256, 256)

    def kernel_c(*refs):
        solve(math.sqrt(total_rows), *refs)

    updated, loadings = pl.pallas_call(
        kernel_c,
        name="solve",
        out_shape=(jax.ShapeDtypeStruct((1024, 256), F32), jax.ShapeDtypeStruct((3, 1024, 256), F32)),
        in_specs=[hbm, hbm, hbm],
        out_specs=(hbm, hbm),
        scratch_shapes=[buf(256, 256), buf(256, 256), buf(1024, 256), buf(3, 1024, 256), buf(1024, 256),
                        pltpu.SemaphoreType.DMA((8,))],
        compiler_params=pltpu.CompilerParams(vmem_limit_bytes=58 * 2**20),
    )(gram, merged, loadings)
    return (loadings, updated)


def solution(mesh):
    return jax.shard_map(
        shards,
        mesh=mesh,
        in_specs=(P("view", "sent", "col"), P("view"), P("view", "sent", "col"), P("sent", None)),
        out_specs=(P("view", "col", None), P("sent", None)),
        check_vma=False,
    )
```
